32 devices in a mesh: row: 8 (over y, x, core), col: 4 (over z).
Axes of the slice: x: 2, y: 2, z: 4, core: 2. Of those that a mesh axis runs over, the one named last changes fastest.
Arguments:
- block_vecs: float32 [16, 16384], P(None, ('col', 'row')), may hold values from -130 to 130
- direction: float32 [16, 16384], P(None, ('col', 'row')), may hold values from -130 to 130
- blocks: bfloat16 [128, 16, 128, 128], P('col', 'row'), may hold values from 0 to 4
- block_cols: int32 [128, 16], P('col', 'row'), may hold values from 0 to 127, as said below
- live_counts: int32 [128, 8], P('col', 'row'), may hold values from 1 to 2, as said below
Outputs:
- x_next: float32 [16, 16384], P(None, ('col', 'row'))
- reduced: float32 [48, 48], replicated
- residual: float32 [16, 16384], P(None, ('col', 'row'))
The draws below stay inside these ranges and needn't reach their ends.
Inputs may be any that keep to these rules, and one draw needn't show every extreme that they name: `block_cols`: A block column index g in slots 2 * r to 2 * r + 1 of any block row satisfies (g // 4) mod 8 == r. `live_counts`: every block row has 2 live slots in at least one segment.
All inputs are finite; a program needn't handle non-finite values.
Results may differ from the reference program's by a relative error of at most 0.0003.
Values sent between devices are 32-bit elements; how exact they have to be, the bound alone decides.
No kernel may reach another device: no remote copies, remote signals or barrier semaphores. Data moves between devices by JAX's collectives and lax.ppermute only.
A program may use at most 64 MiB of HBM per device.

```python
import math
import jax
import jax.numpy as jnp
from jax import lax

W = 16
BS = 128
KT = 2
M = 512
ORDER = 16384
NBR = 128
N_ROW = 8
N_COL = 4


def vector_draw(key):
    subkeys = jax.random.split(key, 3)
    position = jnp.arange(ORDER, dtype=jnp.float32) / ORDER
    rough = jax.random.uniform(subkeys[0], (ORDER,), jnp.float32)
    row_scale = 10.0 ** (0.5 * position + 0.5 * rough)
    col_scale = 10.0 ** (0.5 * jax.random.uniform(subkeys[1], (W, 1), jnp.float32))
    base = jax.random.normal(subkeys[2], (W, ORDER), jnp.float32)
    base = jnp.clip(base, -4.0, 4.0)
    return base * row_scale[None, :] * col_scale


def draw_block_vecs(key, part):
    return vector_draw(jax.random.fold_in(key, 11))


def draw_direction(key, part):
    return vector_draw(jax.random.fold_in(key, 23))


def draw_blocks(key, part):
    fan_total = BS * KT * N_ROW
    levels = jax.random.uniform(jax.random.fold_in(key, 71), (NBR, N_ROW * KT, BS, BS), jnp.float32)
    return (0.04 / math.sqrt(fan_total) * 100.0 ** levels).astype(jnp.bfloat16)


def draw_block_cols(key, part):
    subkeys = jax.random.split(jax.random.fold_in(key, 37), 4)
    per_span = M // BS
    slot_count = N_ROW * KT
    segment = jnp.arange(slot_count, dtype=jnp.int32) // KT
    group_index = jax.random.randint(subkeys[0], (NBR, slot_count), 0, N_COL)
    offset = jax.random.randint(subkeys[1], (NBR, slot_count), 0, per_span)
    columns = (group_index * N_ROW + segment[None, :]) * per_span + offset
    low_row = jax.random.randint(subkeys[2], (), 0, NBR)
    high_row = jax.random.randint(subkeys[3], (), 0, NBR)
    columns = columns.at[low_row, 0].set(0)
    columns = columns.at[high_row, slot_count - 1].set(NBR - 1)
    return columns.astype(jnp.int32)


def draw_live_counts(key, part):
    subkeys = jax.random.split(jax.random.fold_in(key, 53), 3)
    counts = jax.random.randint(subkeys[0], (NBR, N_ROW), 1, KT + 1)
    full_segment = jax.random.randint(subkeys[1], (NBR,), 0, N_ROW)
    segment = jnp.arange(N_ROW, dtype=jnp.int32)[None, :]
    counts = jnp.where(segment == full_segment[:, None], KT, counts)
    single_row = jax.random.randint(subkeys[2], (), 0, NBR)
    counts = counts.at[single_row, (full_segment[single_row] + 1) % N_ROW].set(1)
    return counts.astype(jnp.int32)


def setup_inputs(seed: int = 0) -> dict:
    key_of = jax.random.split(jax.random.key(seed), 6)
    block_vecs = draw_block_vecs(jax.random.fold_in(key_of[5], 71), 0)
    direction = draw_direction(jax.random.fold_in(key_of[5], 71), 0)
    blocks = draw_blocks(jax.random.fold_in(key_of[5], 71), 0)
    block_cols = draw_block_cols(jax.random.fold_in(key_of[5], 71), 0)
    live_counts = draw_live_counts(jax.random.fold_in(key_of[5], 71), 0)
    return dict(block_vecs=block_vecs, direction=direction, blocks=blocks, block_cols=block_cols, live_counts=live_counts)


highest = lax.Precision.HIGHEST

def outer(left, right):
    return jnp.dot(left.astype(jnp.float32), right.T.astype(jnp.float32), precision=highest, preferred_element_type=jnp.float32)

def apply_matrix(vectors, blocks, block_cols, live_counts):
    vec_width = vectors.shape[0]
    block_rows = blocks.shape[0]
    slot_count = blocks.shape[1]
    block_size = blocks.shape[2]
    source = vectors.reshape(vec_width, block_rows, block_size)
    live_mask = ((jnp.arange(slot_count, dtype=jnp.int32) % KT)[None, :] < jnp.repeat(live_counts, KT, axis=1)).astype(jnp.float32)

    def one_slot(slot, carry):
        forward, backward = carry
        block_tile = lax.dynamic_index_in_dim(blocks, slot, 1, keepdims=False).astype(jnp.float32)
        target = lax.dynamic_index_in_dim(block_cols, slot, 1, keepdims=False)
        weight = lax.dynamic_index_in_dim(live_mask, slot, 1, keepdims=False)
        picked = source[:, target, :] * weight[None, :, None]
        forward = forward + jnp.einsum('vbj,bij->vbi', picked, block_tile, precision=highest)
        spread = jnp.einsum('vbi,bij->vbj', source, block_tile, precision=highest) * weight[None, :, None]
        backward = backward.at[:, target, :].add(spread)
        return (forward, backward)
    empty_acc = jnp.zeros((vec_width, block_rows, block_size), jnp.float32)
    forward, backward = lax.fori_loop(0, slot_count, one_slot, (empty_acc, empty_acc))
    return (0.5 * (forward + backward)).reshape(vec_width, -1)

def reference(block_vecs, direction, blocks, block_cols, live_counts):
    paired = jnp.concatenate([block_vecs, direction], axis=0)
    image_pair = apply_matrix(paired, blocks, block_cols, live_counts)
    image_x = image_pair[:W]
    image_p = image_pair[W:]
    gram_x = outer(block_vecs, block_vecs)
    cross_x = outer(block_vecs, image_x)
    factor_x = jnp.linalg.cholesky(gram_x)
    coefficient = jax.scipy.linalg.cho_solve((factor_x, True), cross_x)
    resid = image_x - jnp.dot(coefficient.T.astype(jnp.float32), block_vecs.astype(jnp.float32), precision=highest, preferred_element_type=jnp.float32)
    image_r = apply_matrix(resid, blocks, block_cols, live_counts)
    basis = jnp.concatenate([block_vecs, resid, direction], axis=0)
    basis_image = jnp.concatenate([image_x, image_r, image_p], axis=0)
    gram_basis = outer(basis, basis)
    gram_apply = outer(basis, basis_image)
    factor = jnp.linalg.cholesky(gram_basis)
    halfway = jax.scipy.linalg.solve_triangular(factor, 0.5 * (gram_apply + gram_apply.T), lower=True)
    reduced = jax.scipy.linalg.solve_triangular(factor, halfway.T, lower=True)
    shifted = reduced + 3.0 * jnp.eye(3 * W, dtype=jnp.float32)
    target = jnp.dot(shifted.astype(jnp.float32), shifted[:, :W].astype(jnp.float32), precision=highest, preferred_element_type=jnp.float32)
    mixing = jax.scipy.linalg.solve_triangular(factor.T, target, lower=False)
    fresh = jnp.dot(mixing.T.astype(jnp.float32), basis.astype(jnp.float32), precision=highest, preferred_element_type=jnp.float32)
    factor_fresh = jnp.linalg.cholesky(outer(fresh, fresh))
    x_next = math.sqrt(ORDER) * jax.scipy.linalg.solve_triangular(factor_fresh, fresh, lower=True)
    return (x_next, reduced, resid)
```

```python
import functools
import math

import jax
import jax.numpy as jnp
from jax import lax
from jax.experimental import pallas as pl
from jax.experimental.pallas import tpu as pltpu
from jax.sharding import PartitionSpec as P

highest = lax.Precision.HIGHEST
f32 = jnp.float32
bf16 = jnp.bfloat16
VMEM = pltpu.MemorySpace.VMEM
SMEM = pltpu.MemorySpace.SMEM
LANES = 128


def dot_nt(a, b, precision=highest):
    return lax.dot_general(
        a, b, (((1,), (1,)), ((), ())), precision=precision, preferred_element_type=f32
    )


def dot_nn(a, b, precision=highest):
    return lax.dot_general(
        a, b, (((1,), (0,)), ((), ())), precision=precision, preferred_element_type=f32
    )


def dot_tn(a, b, precision=highest):
    return lax.dot_general(
        a, b, (((0,), (0,)), ((), ())), precision=precision, preferred_element_type=f32
    )


def split(x):
    hi = x.astype(bf16)
    lo = (x - hi.astype(f32)).astype(bf16)
    return hi, lo


def split_rows(x):
    hi, lo = split(x)
    return jnp.concatenate([hi, lo], axis=0)


def eye(n):
    return (
        lax.broadcasted_iota(jnp.int32, (n, n), 0) == lax.broadcasted_iota(jnp.int32, (n, n), 1)
    ).astype(f32)


def eliminate(stack, n):
    m = stack.shape[1]
    row_at = lax.broadcasted_iota(jnp.int32, (n, m), 0)
    lane_at = lax.broadcasted_iota(jnp.int32, (n, m), 1)
    for j in range(n - 1):
        row = stack[j : j + 1, :]
        pivot = stack[j : j + 1, j : j + 1]
        column = jnp.broadcast_to(stack[:, j : j + 1], (n, m))
        scaled = row / pivot
        stack = stack - jnp.where(row_at > j, column, 0.0) * scaled
    diagonal = jnp.sum(jnp.where(row_at == lane_at, stack, 0.0), axis=1, keepdims=True)
    return stack / jnp.sqrt(diagonal)


def place(block_cols_ref, b, k, me_col, per_span, row_count):
    g = block_cols_ref[b, k]
    span = lax.div(g, per_span)
    return (lax.div(span, row_count) ^ me_col) * per_span + lax.rem(g, per_span)


def first_kernel(
    row_count, col_count, slots, width, bs,
    block_cols_ref, live_ref, rows_ref, *rest,
):
    col_refs = rest[:col_count]
    blocks_ref = rest[col_count]
    fr_ref, fp_ref = rest[col_count + 1 : col_count + 3]
    bk_refs = rest[col_count + 3 : 2 * col_count + 3]
    picks, spread = rest[2 * col_count + 3 :]
    span_rows = rows_ref.shape[2]
    per_span = span_rows // bs
    me_col = lax.axis_index("col")
    for s in range(col_count):
        for o in range(per_span):
            picks[s * per_span + o] = split_rows(col_refs[s][:, o * bs : (o + 1) * bs])
    spread[...] = jnp.zeros_like(spread)

    def span_step(q, cross):
        panel = rows_ref[q]
        own = split_rows(panel[:width])
        parts = []
        for o in range(per_span):
            b = q * per_span + o
            tiles, chosen, weights, where = [], [], [], []
            for k in range(slots):
                w = (k < live_ref[b, 0]).astype(f32)
                at = place(block_cols_ref, b, k, me_col, per_span, row_count)
                tiles.append(blocks_ref[b, k])
                chosen.append(picks[at] * w.astype(bf16))
                weights.append(w)
                where.append(at)
            tile = jnp.concatenate(tiles, axis=1)
            forward = dot_nt(jnp.concatenate(chosen, axis=1), tile, None)
            parts.append(forward[: 2 * width] + forward[2 * width :])
            back = dot_nn(own[:, o * bs : (o + 1) * bs], tile, None)
            back = back[:width] + back[width:]
            for k in range(slots):
                spread[where[k]] += back[:, k * bs : (k + 1) * bs] * weights[k]
        forward = jnp.concatenate(parts, axis=1)
        fr_ref[q, :, :span_rows] = forward[:width]
        fp_ref[q] = forward[width:]
        return cross + dot_nt(panel, forward)

    cross = lax.fori_loop(0, row_count, span_step, jnp.zeros((2 * width, 2 * width), f32))
    gram = dot_nt(col_refs[0][...], col_refs[0][...])
    extra = jnp.concatenate([gram[:width], gram[width:], cross[:width], cross[width:]], axis=1)
    for q in range(row_count):
        fr_ref[q, :, span_rows:] = extra
    for s in range(col_count):
        for o in range(per_span):
            bk_refs[s][:, o * bs : (o + 1) * bs] = spread[s * per_span + o]


def middle_kernel(row_count, col_count, got_ref, *rest):
    back_refs = rest[:col_count]
    out_ref, y_ref = rest[col_count:]
    span_rows = y_ref.shape[1]
    total = got_ref[0]
    for q in range(1, row_count):
        total = total + got_ref[q]
    back = back_refs[0][...]
    for s in range(1, col_count):
        back = back + back_refs[s][...]
    y = 0.5 * (total[:, :span_rows] + back)
    y_ref[...] = y
    out_ref[:, :span_rows] = y
    out_ref[:, span_rows:] = total[:, span_rows:]


def tree_sum(terms):
    while len(terms) > 1:
        terms = [terms[i] + terms[i + 1] for i in range(0, len(terms), 2)]
    return terms[0]


def second_kernel(
    row_count, col_count, slots, width, bs,
    block_cols_ref, live_ref, rows_ref, fp_ref, yrows_ref, *rest,
):
    col_refs = rest[:col_count]
    y_refs = rest[col_count : 2 * col_count]
    blocks_ref = rest[2 * col_count]
    resid_ref, part_ref, aux_ref = rest[2 * col_count + 1 : 2 * col_count + 4]
    picks, forward_r, resid_rows = rest[2 * col_count + 4 :]
    span_rows = rows_ref.shape[2]
    per_span = span_rows // bs
    me_col = lax.axis_index("col")
    me_row = lax.axis_index("row")

    sums = tree_sum([y_refs[s][:, span_rows:] for s in range(col_count)])
    gram_x = sums[:, :width]
    cross_x = sums[:, 4 * width : 5 * width]
    cross_x = 0.5 * (cross_x + cross_x.T)
    done = eliminate(jnp.concatenate([gram_x, cross_x, eye(width)], axis=1), width)
    inverse_l = done[:, 2 * width : 3 * width]
    coefficient = dot_tn(inverse_l, done[:, width : 2 * width])
    minus_c_t = -coefficient.T
    aux_ref[:, : sums.shape[1]] = sums
    aux_ref[:, sums.shape[1] :] = jnp.concatenate(
        [coefficient, jnp.zeros((width, sums.shape[1] - width), f32)], axis=1
    )
    for s in range(col_count):
        rest_s = y_refs[s][:, :span_rows] + dot_nn(minus_c_t, col_refs[s][:width, :])
        for o in range(per_span):
            picks[s * per_span + o] = split_rows(rest_s[:, o * bs : (o + 1) * bs])

    def span_step(q, carry):
        own, cross = carry
        rest_q = yrows_ref[q] + dot_nn(minus_c_t, rows_ref[q, :width, :])
        resid_rows[q] = rest_q
        parts = []
        for o in range(per_span):
            b = q * per_span + o
            tiles, chosen = [], []
            for k in range(slots):
                w = (k < live_ref[b, 0]).astype(f32)
                at = place(block_cols_ref, b, k, me_col, per_span, row_count)
                tiles.append(blocks_ref[b, k])
                chosen.append(picks[at] * w.astype(bf16))
            forward = dot_nt(
                jnp.concatenate(chosen, axis=1), jnp.concatenate(tiles, axis=1), None
            )
            parts.append(forward[:width] + forward[width:])
        forward = jnp.concatenate(parts, axis=1)
        own = own + dot_nt(forward, rest_q)
        cross = cross + dot_nt(forward, rows_ref[q, width:, :]) + dot_nt(rest_q, fp_ref[q])
        return own, cross

    zero = jnp.zeros((width, width), f32)
    own, cross = lax.fori_loop(0, row_count, span_step, (zero, zero))
    mine = resid_rows[me_row]
    resid_ref[...] = mine
    local = jnp.concatenate([col_refs[0][:width, :], mine, col_refs[0][width:, :]], axis=0)
    part = jnp.concatenate(
        [dot_nt(mine, local), own, 0.5 * cross, jnp.zeros((width, LANES - 5 * width), f32)],
        axis=1,
    )
    for d in range(part_ref.shape[0]):
        part_ref[d] = part


def last_kernel(width, scale, parts_ref, aux_ref, xp_ref, resid_ref, x_next_ref, reduced_ref):
    w = width
    total = parts_ref[0]
    for d in range(1, parts_ref.shape[0]):
        total = total + parts_ref[d]
    sums = aux_ref[:, :LANES]
    coefficient = aux_ref[:, LANES : LANES + w]
    piece = lambda array, i: array[:, i * w : (i + 1) * w]
    xx, xp, pp = piece(sums, 0), piece(sums, 1), piece(sums, 3)
    xbx, xbp, pbx, pbp = (piece(sums, i) for i in range(4, 8))
    rx, rr, rp, rbr, rap = (piece(total, i) for i in range(5))
    xr = rx.T
    gram_basis = jnp.concatenate(
        [
            jnp.concatenate([xx, xr, xp], axis=1),
            jnp.concatenate([rx, rr, rp], axis=1),
            jnp.concatenate([xp.T, rp.T, pp], axis=1),
        ],
        axis=0,
    )
    xax = 0.5 * (xbx + xbx.T)
    xap = 0.5 * (xbp + pbx.T)
    xar = rr + dot_tn(coefficient, xr)
    gram_apply = jnp.concatenate(
        [
            jnp.concatenate([xax, xar, xap], axis=1),
            jnp.concatenate([xar.T, 0.5 * (rbr + rbr.T), rap], axis=1),
            jnp.concatenate([xap.T, rap.T, 0.5 * (pbp + pbp.T)], axis=1),
        ],
        axis=0,
    )
    n = 3 * w
    inverse_l = eliminate(jnp.concatenate([gram_basis, eye(n)], axis=1), n)[:, n:]
    reduced = dot_nt(dot_nn(inverse_l, gram_apply), inverse_l)
    reduced_ref[...] = reduced
    shifted = reduced + 3.0 * eye(n)
    target = dot_nn(shifted, shifted[:, :w])
    gram_fresh = dot_tn(target, target)
    mixing = dot_tn(target, inverse_l)
    weights = scale * eliminate(jnp.concatenate([gram_fresh, mixing], axis=1), w)[:, w:]
    basis = jnp.concatenate([xp_ref[:w, :], resid_ref[...], xp_ref[w:, :]], axis=0)
    x_next_ref[...] = dot_nn(weights, basis)


def vmem_specs(n):
    return [pl.BlockSpec(memory_space=VMEM)] * n


def per_device(block_vecs, direction, blocks, block_cols, live_counts):
    row_count = lax.axis_size("row")
    col_count = lax.axis_size("col")
    width, span_rows = block_vecs.shape
    slots, bs = blocks.shape[1], blocks.shape[2]
    per_span = span_rows // bs
    order_total = span_rows * row_count * col_count
    col_blocks = col_count * per_span
    sizes = (row_count, col_count, slots, width, bs)

    def over_col(arrays):
        return [arrays[0]] + [
            lax.ppermute(arrays[s], "col", [(i, i ^ s) for i in range(col_count)])
            for s in range(1, col_count)
        ]

    shape = lambda *dims: jax.ShapeDtypeStruct(dims, f32)
    smem = [pl.BlockSpec(memory_space=SMEM)] * 2
    params = pltpu.CompilerParams(vmem_limit_bytes=48 * 1024 * 1024)

    pair = jnp.concatenate([block_vecs, direction], axis=0)
    pair_cols = over_col([pair] * col_count)
    pair_rows = lax.all_gather(pair, "row")
    first = pl.pallas_call(
        functools.partial(first_kernel, *sizes),
        in_specs=smem + vmem_specs(col_count + 2),
        out_specs=vmem_specs(col_count + 2),
        out_shape=[shape(row_count, width, span_rows + LANES), shape(row_count, width, span_rows)]
        + [shape(width, span_rows)] * col_count,
        scratch_shapes=[
            pltpu.VMEM((col_blocks, 4 * width, bs), bf16),
            pltpu.VMEM((col_blocks, width, bs), f32),
        ],
        compiler_params=params,
        name="first",
    )(block_cols, live_counts, pair_rows, *pair_cols, blocks)
    forward, forward_p, backs = first[0], first[1], first[2:]
    got_backs = over_col(backs)
    got = lax.all_to_all(forward, "row", 0, 0)
    message, image = pl.pallas_call(
        functools.partial(middle_kernel, row_count, col_count),
        in_specs=vmem_specs(col_count + 1),
        out_specs=vmem_specs(2),
        out_shape=[shape(width, span_rows + LANES), shape(width, span_rows)],
        compiler_params=params,
        name="middle",
    )(got, *got_backs)
    image_cols = over_col([message] * col_count)
    image_rows = lax.all_gather(image, "row")
    device_count = row_count * col_count
    resid, part, aux = pl.pallas_call(
        functools.partial(second_kernel, *sizes),
        in_specs=smem + vmem_specs(2 * col_count + 4),
        out_specs=vmem_specs(3),
        out_shape=[
            shape(width, span_rows),
            shape(device_count, width, LANES),
            shape(width, 2 * LANES),
        ],
        scratch_shapes=[
            pltpu.VMEM((col_blocks, 2 * width, bs), bf16),
            pltpu.VMEM((8, LANES), f32),
            pltpu.VMEM((row_count, width, span_rows), f32),
        ],
        compiler_params=params,
        name="second",
    )(block_cols, live_counts, pair_rows, forward_p, image_rows, *pair_cols, *image_cols, blocks)
    parts = lax.all_to_all(part, ("col", "row"), 0, 0)
    x_next, reduced = pl.pallas_call(
        functools.partial(last_kernel, width, math.sqrt(order_total)),
        in_specs=vmem_specs(4),
        out_specs=vmem_specs(2),
        out_shape=[shape(width, span_rows), shape(3 * width, 3 * width)],
        compiler_params=params,
        name="last",
    )(parts, aux, pair, resid)
    return (x_next, reduced, resid)


def solution(mesh):
    return jax.shard_map(
        per_device,
        mesh=mesh,
        in_specs=(
            P(None, ("col", "row")),
            P(None, ("col", "row")),
            P("col", "row", None, None),
            P("col", "row"),
            P("col", "row"),
        ),
        out_specs=(P(None, ("col", "row")), P(), P(None, ("col", "row"))),
        check_vma=False,
    )
```

```python
import functools
import math

import jax
import jax.numpy as jnp
from jax import lax
from jax.experimental import pallas as pl
from jax.experimental.pallas import tpu as pltpu
from jax.sharding import PartitionSpec as P


highest = lax.Precision.HIGHEST
f32 = jnp.float32
bf16 = jnp.bfloat16
VMEM = pltpu.MemorySpace.VMEM
HBM = pltpu.MemorySpace.HBM
LANES = 128
VMEM_LIMIT = 16 * 1024 * 1024


def dot_nt(a, b, precision=highest):
    return lax.dot_general(
        a, b, (((1,), (1,)), ((), ())), precision=precision, preferred_element_type=f32
    )


def dot_nn(a, b, precision=highest):
    return lax.dot_general(
        a, b, (((1,), (0,)), ((), ())), precision=precision, preferred_element_type=f32
    )


def dot_tn(a, b, precision=highest):
    return lax.dot_general(
        a, b, (((0,), (0,)), ((), ())), precision=precision, preferred_element_type=f32
    )


def split(x):
    hi = x.astype(bf16)
    lo = (x - hi.astype(f32)).astype(bf16)
    return hi, lo


def split_rows(x):
    hi, lo = split(x)
    return jnp.concatenate([hi, lo], axis=0)


def eye(n):
    return (
        lax.broadcasted_iota(jnp.int32, (n, n), 0) == lax.broadcasted_iota(jnp.int32, (n, n), 1)
    ).astype(f32)


def eliminate(stack, n):
    m = stack.shape[1]
    row_at = lax.broadcasted_iota(jnp.int32, (n, m), 0)
    lane_at = lax.broadcasted_iota(jnp.int32, (n, m), 1)
    for j in range(n - 1):
        row = stack[j : j + 1, :]
        pivot = stack[j : j + 1, j : j + 1]
        column = jnp.broadcast_to(stack[:, j : j + 1], (n, m))
        scaled = row / pivot
        stack = stack - jnp.where(row_at > j, column, 0.0) * scaled
    diagonal = jnp.sum(jnp.where(row_at == lane_at, stack, 0.0), axis=1, keepdims=True)
    return stack / jnp.sqrt(diagonal)


def tree_sum(terms):
    while len(terms) > 1:
        terms = [terms[i] + terms[i + 1] for i in range(0, len(terms), 2)]
    return terms[0]


def place(block_cols_ref, b, k, me_col, per_span, row_count):
    g = block_cols_ref[k, b]
    span = lax.div(g, per_span)
    return (lax.div(span, row_count) ^ me_col) * per_span + lax.rem(g, per_span)


def pair_kernel(x_hbm, p_hbm, out_ref, sems):
    w = x_hbm.shape[0]
    copies = [
        pltpu.make_async_copy(x_hbm, out_ref.at[:w], sems.at[0]),
        pltpu.make_async_copy(p_hbm, out_ref.at[w:], sems.at[1]),
    ]
    for copy in copies:
        copy.start()
    for copy in copies:
        copy.wait()


def first_kernel(
    row_count, col_count, slots, width, bs,
    cols_hbm, live_hbm, even_ref, odd_ref, *rest,
):
    col_refs = rest[:col_count]
    blocks_hbm = rest[col_count]
    keep_ref, send_ref, fp_ref = rest[col_count + 1 : col_count + 4]
    bk_refs = rest[col_count + 4 : 2 * col_count + 4]
    picks, spread, blocks_ref, block_cols_ref, live_ref, sems, small_sems = rest[2 * col_count + 4 :]
    span_rows = even_ref.shape[2]
    per_span = span_rows // bs
    half = row_count // 2
    me_col = lax.axis_index("col")
    me_row = lax.axis_index("row")

    def fetch(s):
        at = pl.ds(pl.multiple_of((me_row ^ s) * per_span, per_span), per_span)
        return pltpu.make_async_copy(blocks_hbm.at[at], blocks_ref.at[at], sems.at[s])

    index_copies = [
        pltpu.make_async_copy(cols_hbm, block_cols_ref, small_sems.at[0]),
        pltpu.make_async_copy(live_hbm, live_ref, small_sems.at[1]),
    ]
    for copy in index_copies:
        copy.start()
    for s in range(row_count):
        fetch(s).start()
    for s in range(col_count):
        for o in range(per_span):
            picks[s * per_span + o] = split_rows(col_refs[s][:, o * bs : (o + 1) * bs])
    spread[...] = jnp.zeros_like(spread)
    for copy in index_copies:
        copy.wait()

    def span_step(s, panel):
        fetch(s).wait()
        q = me_row ^ s
        own = split_rows(panel[:width])
        parts = []
        for o in range(per_span):
            b = q * per_span + o
            tiles, chosen, weights, where = [], [], [], []
            for k in range(slots):
                w = (k < live_ref[0, b]).astype(f32)
                at = place(block_cols_ref, b, k, me_col, per_span, row_count)
                tiles.append(blocks_ref[b, k])
                chosen.append(picks[at] * w.astype(bf16))
                weights.append(w)
                where.append(at)
            tile = jnp.concatenate(tiles, axis=1)
            forward = dot_nt(jnp.concatenate(chosen, axis=1), tile, None)
            parts.append(forward[: 2 * width] + forward[2 * width :])
            back = dot_nn(own[:, o * bs : (o + 1) * bs], tile, None)
            back = back[:width] + back[width:]
            for k in range(slots):
                spread[where[k]] += back[:, k * bs : (k + 1) * bs] * weights[k]
        forward = jnp.concatenate(parts, axis=1)
        fp_ref[s] = forward[width:]
        return forward[:width], dot_nt(panel, forward)

    def two_spans(h, cross):
        keep, c0 = span_step(2 * h, even_ref[h])
        send, c1 = span_step(2 * h + 1, odd_ref[h])
        keep_ref[h, :, :span_rows] = keep
        send_ref[h, :, :span_rows] = send
        return cross + c0 + c1

    cross = lax.fori_loop(0, half, two_spans, jnp.zeros((2 * width, 2 * width), f32))
    gram = dot_nt(col_refs[0][...], col_refs[0][...])
    extra = jnp.concatenate([gram[:width], gram[width:], cross[:width], cross[width:]], axis=1)
    for h in range(half):
        keep_ref[h, :, span_rows:] = extra
        send_ref[h, :, span_rows:] = extra
    for s in range(col_count):
        for o in range(per_span):
            bk_refs[s][:, o * bs : (o + 1) * bs] = spread[s * per_span + o]


def fold_kernel(keep_ref, got_ref, *out_refs):
    for h, out_ref in enumerate(out_refs):
        out_ref[...] = keep_ref[h] + got_ref[h]


def middle_kernel(half, col_count, *refs):
    row_refs = refs[:half]
    back_refs = refs[half : half + col_count]
    out_ref, y_ref = refs[half + col_count :]
    span_rows = y_ref.shape[1]
    total = tree_sum([ref[...] for ref in row_refs])
    back = tree_sum([ref[...] for ref in back_refs])
    y = 0.5 * (total[:, :span_rows] + back)
    y_ref[...] = y
    out_ref[:, :span_rows] = y
    out_ref[:, span_rows:] = total[:, span_rows:]


def pack(matrices):
    h = matrices[0].shape[0] // 2
    return jnp.concatenate([part for m in matrices for part in (m[:h], m[h:])], axis=1)


def unpack(packed, i):
    w = 2 * packed.shape[0]
    at = 2 * i * w
    return jnp.concatenate([packed[:, at : at + w], packed[:, at + w : at + 2 * w]], axis=0)


def second_kernel(
    row_count, col_count, slots, width, bs,
    cols_hbm, live_hbm, even_ref, odd_ref, fp_ref, yeven_ref, yodd_ref, *rest,
):
    col_refs = rest[:col_count]
    y_refs = rest[col_count : 2 * col_count]
    blocks_ref = rest[2 * col_count]
    resid_ref, part_ref, aux_ref = rest[2 * col_count + 1 : 2 * col_count + 4]
    picks, block_cols_ref, live_ref, small_sems = rest[2 * col_count + 4 :]
    span_rows = even_ref.shape[2]
    per_span = span_rows // bs
    half = row_count // 2
    me_col = lax.axis_index("col")
    me_row = lax.axis_index("row")
    index_copies = [
        pltpu.make_async_copy(cols_hbm, block_cols_ref, small_sems.at[0]),
        pltpu.make_async_copy(live_hbm, live_ref, small_sems.at[1]),
    ]
    for copy in index_copies:
        copy.start()

    sums = tree_sum([y_refs[s][:, span_rows:] for s in range(col_count)])
    gram_x = sums[:, :width]
    cross_x = sums[:, 4 * width : 5 * width]
    cross_x = 0.5 * (cross_x + cross_x.T)
    done = eliminate(jnp.concatenate([gram_x, cross_x, eye(width)], axis=1), width)
    inverse_l = done[:, 2 * width : 3 * width]
    coefficient = dot_tn(inverse_l, done[:, width : 2 * width])
    minus_c_t = -coefficient.T
    x_resid = cross_x - dot_nn(gram_x, coefficient)
    aux_ref[:, : sums.shape[1]] = sums
    aux_ref[:, sums.shape[1] :] = jnp.concatenate(
        [coefficient, x_resid, jnp.zeros((width, sums.shape[1] - 2 * width), f32)], axis=1
    )
    for s in range(col_count):
        rest_s = y_refs[s][:, :span_rows] + dot_nn(minus_c_t, col_refs[s][:width, :])
        for o in range(per_span):
            picks[s * per_span + o] = split_rows(rest_s[:, o * bs : (o + 1) * bs])
    mine = y_refs[0][:, :span_rows] + dot_nn(minus_c_t, col_refs[0][:width, :])
    resid_ref[...] = mine
    for copy in index_copies:
        copy.wait()

    def span_step(s, panel, image):
        q = me_row ^ s
        rest_q = image + dot_nn(minus_c_t, panel[:width])
        parts = []
        for o in range(per_span):
            b = q * per_span + o
            tiles, chosen = [], []
            for k in range(slots):
                w = (k < live_ref[0, b]).astype(f32)
                at = place(block_cols_ref, b, k, me_col, per_span, row_count)
                tiles.append(blocks_ref[b, k])
                chosen.append(picks[at] * w.astype(bf16))
            forward = dot_nt(
                jnp.concatenate(chosen, axis=1), jnp.concatenate(tiles, axis=1), None
            )
            parts.append(forward[:width] + forward[width:])
        forward = jnp.concatenate(parts, axis=1)
        own = dot_nt(forward, rest_q)
        cross = dot_nt(forward, panel[width:]) + dot_nt(rest_q, fp_ref[s])
        return own, cross

    def two_spans(h, carry):
        own, cross = carry
        own0, cross0 = span_step(2 * h, even_ref[h], yeven_ref[h])
        own1, cross1 = span_step(2 * h + 1, odd_ref[h], yodd_ref[h])
        return own + own0 + own1, cross + cross0 + cross1

    zero = jnp.zeros((width, width), f32)
    own, cross = lax.fori_loop(0, half, two_spans, (zero, zero))
    local = jnp.concatenate([mine, col_refs[0][width:, :]], axis=0)
    gram = dot_nt(mine, local)
    part = pack([gram[:, :width], gram[:, width:], own, 0.5 * cross])
    for d in range(part_ref.shape[0]):
        part_ref[d] = part


def last_kernel(
    width, scale, parts_ref, aux_ref, xp_ref, resid_hbm, x_next_ref, reduced_ref, resid_ref, sem
):
    w = width
    fetch = pltpu.make_async_copy(resid_hbm, resid_ref, sem)
    fetch.start()
    total = parts_ref[0]
    for d in range(1, parts_ref.shape[0]):
        total = total + parts_ref[d]
    piece = lambda i: aux_ref[:, i * w : (i + 1) * w]
    per = LANES // w
    xx, xp, pp = piece(0), piece(1), piece(3)
    xbx, xbp, pbx, pbp = (piece(i) for i in range(4, 8))
    coefficient, xr = piece(per), piece(per + 1)
    rr, rp, rbr, rap = (unpack(total, i) for i in range(4))
    gram_basis = jnp.concatenate(
        [
            jnp.concatenate([xx, xr, xp], axis=1),
            jnp.concatenate([xr.T, rr, rp], axis=1),
            jnp.concatenate([xp.T, rp.T, pp], axis=1),
        ],
        axis=0,
    )
    xax = 0.5 * (xbx + xbx.T)
    xap = 0.5 * (xbp + pbx.T)
    xar = rr + dot_tn(coefficient, xr)
    gram_apply = jnp.concatenate(
        [
            jnp.concatenate([xax, xar, xap], axis=1),
            jnp.concatenate([xar.T, 0.5 * (rbr + rbr.T), rap], axis=1),
            jnp.concatenate([xap.T, rap.T, 0.5 * (pbp + pbp.T)], axis=1),
        ],
        axis=0,
    )
    n = 3 * w
    inverse_l = eliminate(jnp.concatenate([gram_basis, eye(n)], axis=1), n)[:, n:]
    reduced = dot_nt(dot_nn(inverse_l, gram_apply), inverse_l)
    reduced_ref[...] = reduced
    shifted = reduced + 3.0 * eye(n)
    target = dot_nn(shifted, shifted[:, :w])
    gram_fresh = dot_tn(target, target)
    mixing = dot_tn(target, inverse_l)
    weights = scale * eliminate(jnp.concatenate([gram_fresh, mixing], axis=1), w)[:, w:]
    fetch.wait()
    basis = jnp.concatenate([xp_ref[:w, :], resid_ref[...], xp_ref[w:, :]], axis=0)
    x_next_ref[...] = dot_nn(weights, basis)


def vmem_specs(n):
    return [pl.BlockSpec(memory_space=VMEM)] * n


def hbm_specs(n):
    return [pl.BlockSpec(memory_space=HBM)] * n


def per_device(block_vecs, direction, blocks, block_cols, live_counts):
    row_count = lax.axis_size("row")
    col_count = lax.axis_size("col")
    width, span_rows = block_vecs.shape
    _, slots, bs = blocks.shape[:3]
    per_span = span_rows // bs
    half = row_count // 2
    order_total = span_rows * row_count * col_count
    col_blocks = col_count * per_span
    sizes = (row_count, col_count, slots, width, bs)
    shape = lambda *dims: jax.ShapeDtypeStruct(dims, f32)
    params = pltpu.CompilerParams(vmem_limit_bytes=VMEM_LIMIT)

    in_hbm = lambda array: pltpu.with_memory_space_constraint(array, HBM)
    blocks_hbm, block_cols, live_counts = map(in_hbm, (blocks, block_cols.T, live_counts.T))

    def swap(array, axis, s):
        return lax.ppermute(array, axis, [(i, i ^ s) for i in range(lax.axis_size(axis))])

    far = list(reversed(range(1, col_count)))
    across = list(reversed(range(2, row_count, 2)))

    def gather(array, array_col):
        rows = {s: swap(array, "row", s) for s in across}
        cols = {s: swap(array_col, "col", s) for s in far}
        even = jnp.stack([array] + [rows[s] for s in range(2, row_count, 2)])
        odd = swap(even, "row", 1)
        return even, odd, [array_col] + [cols[s] for s in range(1, col_count)]

    index_scratch = [
        pltpu.SMEM(block_cols.shape, jnp.int32),
        pltpu.SMEM(live_counts.shape, jnp.int32),
    ]
    pair = pl.pallas_call(
        pair_kernel,
        in_specs=hbm_specs(2),
        scratch_shapes=[pltpu.SemaphoreType.DMA((2,))],
        out_specs=vmem_specs(1)[0],
        out_shape=shape(2 * width, span_rows),
        compiler_params=params,
        name="pair",
    )(in_hbm(block_vecs), in_hbm(direction))
    pair_even, pair_odd, pair_cols = gather(pair, pair)
    first = pl.pallas_call(
        functools.partial(first_kernel, *sizes),
        in_specs=hbm_specs(2) + vmem_specs(col_count + 2) + hbm_specs(1),
        out_specs=vmem_specs(col_count + 3),
        out_shape=[shape(half, width, span_rows + LANES)] * 2
        + [shape(row_count, width, span_rows)]
        + [shape(width, span_rows)] * col_count,
        scratch_shapes=[
            pltpu.VMEM((col_blocks, 4 * width, bs), bf16),
            pltpu.VMEM((col_blocks, width, bs), f32),
            pltpu.VMEM(blocks.shape, bf16),
        ]
        + index_scratch
        + [pltpu.SemaphoreType.DMA((row_count,)), pltpu.SemaphoreType.DMA((2,))],
        compiler_params=params,
        name="first",
    )(block_cols, live_counts, pair_even, pair_odd, *pair_cols, blocks_hbm)
    keep, send, forward_p, backs = first[0], first[1], first[2], first[3:]
    got_pair = swap(send, "row", 1)
    got_backs = {s: swap(backs[s], "col", s) for s in far}
    folded = pl.pallas_call(
        fold_kernel,
        in_specs=vmem_specs(2),
        out_specs=vmem_specs(half),
        out_shape=[shape(width, span_rows + LANES)] * half,
        compiler_params=params,
        name="fold",
    )(keep, got_pair)
    got_rows = {s: swap(folded[s // 2], "row", s) for s in across}
    message, image = pl.pallas_call(
        functools.partial(middle_kernel, half, col_count),
        in_specs=vmem_specs(half + col_count),
        out_specs=vmem_specs(2),
        out_shape=[shape(width, span_rows + LANES), shape(width, span_rows)],
        compiler_params=params,
        name="middle",
    )(
        folded[0],
        *[got_rows[s] for s in range(2, row_count, 2)],
        backs[0],
        *[got_backs[s] for s in range(1, col_count)],
    )
    image_even, image_odd, image_cols = gather(image, message)
    device_count = row_count * col_count
    resid, part, aux = pl.pallas_call(
        functools.partial(second_kernel, *sizes),
        in_specs=hbm_specs(2) + vmem_specs(2 * col_count + 6),
        out_specs=vmem_specs(3),
        out_shape=[
            shape(width, span_rows),
            shape(device_count, width // 2, LANES),
            shape(width, 2 * LANES),
        ],
        scratch_shapes=[pltpu.VMEM((col_blocks, 2 * width, bs), bf16)]
        + index_scratch
        + [pltpu.SemaphoreType.DMA((2,))],
        compiler_params=params,
        name="second",
    )(
        block_cols, live_counts, pair_even, pair_odd, forward_p, image_even, image_odd,
        *pair_cols, *image_cols, blocks,
    )
    parts = lax.all_to_all(part, ("col", "row"), 0, 0)
    x_next, reduced = pl.pallas_call(
        functools.partial(last_kernel, width, math.sqrt(order_total)),
        in_specs=vmem_specs(3) + hbm_specs(1),
        out_specs=vmem_specs(2),
        out_shape=[shape(width, span_rows), shape(3 * width, 3 * width)],
        scratch_shapes=[pltpu.VMEM((width, span_rows), f32), pltpu.SemaphoreType.DMA(())],
        compiler_params=params,
        name="last",
    )(parts, aux, pair, in_hbm(resid))
    return (x_next, reduced, resid)


def solution(mesh):
    return jax.shard_map(
        per_device,
        mesh=mesh,
        in_specs=(
            P(None, ("col", "row")),
            P(None, ("col", "row")),
            P("col", "row", None, None),
            P("col", "row"),
            P("col", "row"),
        ),
        out_specs=(P(None, ("col", "row")), P(), P(None, ("col", "row"))),
        check_vma=False,
    )
```

```python
import functools
import math

import jax
import jax.numpy as jnp
from jax import lax
from jax.experimental import pallas as pl
from jax.experimental.pallas import tpu as pltpu
from jax.sharding import PartitionSpec as P


highest = lax.Precision.HIGHEST
f32 = jnp.float32
bf16 = jnp.bfloat16
VMEM = pltpu.MemorySpace.VMEM
HBM = pltpu.MemorySpace.HBM
SMEM = pltpu.MemorySpace.SMEM
LANES = 128
VMEM_LIMIT = 16 * 1024 * 1024
LOAD_FLOPS = 20_000_000_000


def dot_nt(a, b, precision=highest):
    return lax.dot_general(
        a, b, (((1,), (1,)), ((), ())), precision=precision, preferred_element_type=f32
    )


def dot_nn(a, b, precision=highest):
    return lax.dot_general(
        a, b, (((1,), (0,)), ((), ())), precision=precision, preferred_element_type=f32
    )


def dot_tn(a, b, precision=highest):
    return lax.dot_general(
        a, b, (((0,), (0,)), ((), ())), precision=precision, preferred_element_type=f32
    )


def split(x):
    hi = x.astype(bf16)
    lo = (x - hi.astype(f32)).astype(bf16)
    return hi, lo


def split_rows(x):
    hi, lo = split(x)
    return jnp.concatenate([hi, lo], axis=0)


def three_pass(dot, a, b):
    a_hi, a_lo = split(a)
    b_hi, b_lo = split(b)
    n = a.shape[0]
    top = dot(jnp.concatenate([a_hi, a_lo], axis=0), b_hi, None)
    return top[:n] + top[n:] + dot(a_hi, b_lo, None)


def eye(n):
    return (
        lax.broadcasted_iota(jnp.int32, (n, n), 0) == lax.broadcasted_iota(jnp.int32, (n, n), 1)
    ).astype(f32)


def eliminate(stack, n):
    m = stack.shape[1]
    row_at = lax.broadcasted_iota(jnp.int32, (n, m), 0)
    lane_at = lax.broadcasted_iota(jnp.int32, (n, m), 1)
    for j in range(0, n - 2, 2):
        one = jnp.broadcast_to(stack[:, j : j + 1], (n, m))
        two = jnp.broadcast_to(stack[:, j + 1 : j + 2], (n, m))
        a, b, d = one[j : j + 1], two[j : j + 1], two[j + 1 : j + 2]
        row_one, row_two = stack[j : j + 1], stack[j + 1 : j + 2]
        over = 1.0 / (a * d - b * b)
        scaled_one = (d * row_one - b * row_two) * over
        scaled_two = (a * row_two - b * row_one) * over
        below = row_at > j + 1
        stack = (
            stack
            - jnp.where(below, one, 0.0) * scaled_one
            - jnp.where(below, two, 0.0) * scaled_two
        )
    odd = row_at % 2 == 1
    above = jnp.concatenate([stack[n - 1 :], stack[: n - 1]], axis=0)
    pivot = jnp.sum(jnp.where(row_at == lane_at + 1, above, 0.0), axis=1, keepdims=True)
    beside = jnp.sum(jnp.where(row_at == lane_at + 1, stack, 0.0), axis=1, keepdims=True)
    ratio = beside / jnp.where(odd[:, :1], pivot, 1.0)
    stack = jnp.where(odd, stack - ratio * above, stack)
    diagonal = jnp.sum(jnp.where(row_at == lane_at, stack, 0.0), axis=1, keepdims=True)
    return stack / jnp.sqrt(diagonal)


def place(block_cols_ref, b, k, me_col, per_span, row_count):
    g = block_cols_ref[k, b]
    span = lax.div(g, per_span)
    return (lax.div(span, row_count) ^ me_col) * per_span + lax.rem(g, per_span)


def load_kernel(x_hbm, p_hbm, cols_hbm, live_hbm, pair_ref, cols_ref, live_ref, sems):
    w = x_hbm.shape[0]
    copies = [
        pltpu.make_async_copy(x_hbm, pair_ref.at[:w], sems.at[0]),
        pltpu.make_async_copy(p_hbm, pair_ref.at[w:], sems.at[1]),
        pltpu.make_async_copy(cols_hbm, cols_ref, sems.at[2]),
        pltpu.make_async_copy(live_hbm, live_ref, sems.at[3]),
    ]
    for copy in copies:
        copy.start()
    for copy in copies:
        copy.wait()


def forward_kernel(sizes, cols_ref, live_ref, even_ref, odd_ref, *rest):
    row_count, col_count, _, width, bs = sizes
    x_refs = rest[:col_count]
    blocks_ref, keep_ref, send_ref, extra_ref, picks = rest[col_count:]
    per_span = keep_ref.shape[2] // bs
    me_col = lax.axis_index("col")
    me_row = lax.axis_index("row")
    for s in range(col_count):
        for o in range(per_span):
            picks[s * per_span + o] = split_rows(x_refs[s][:width, o * bs : (o + 1) * bs])
    pair = x_refs[0][...]
    gram = dot_nt(pair, pair)

    def two_spans(h, cross):
        for i, (out_ref, rows_ref) in enumerate(((keep_ref, even_ref), (send_ref, odd_ref))):
            forward = forward_span(
                sizes, 2 * h + i, cols_ref, live_ref, picks, blocks_ref, per_span, me_row, me_col
            )
            out_ref[h] = forward
            cross = cross + three_pass(dot_nt, rows_ref[h, :width, :], forward)
        return cross

    cross = lax.fori_loop(0, row_count // 2, two_spans, jnp.zeros((width, width), f32))
    extra_ref[...] = pack([gram[:width, :width], gram[:width, width:], gram[width:, width:], cross])


def forward_span(
    sizes, s, cols_ref, live_ref, picks, blocks_ref, per_span, me_row, me_col
):
    row_count, _, slots, _, _ = sizes
    n = picks.shape[1] // 2
    parts = []
    for o in range(per_span):
        b = (me_row ^ s) * per_span + o
        tiles, chosen = [], []
        for k in range(slots):
            w = (k < live_ref[0, b]).astype(f32)
            at = place(cols_ref, b, k, me_col, per_span, row_count)
            tiles.append(blocks_ref[b, k])
            chosen.append(picks[at] * w.astype(bf16))
        both = dot_nt(jnp.concatenate(chosen, axis=1), jnp.concatenate(tiles, axis=1), None)
        parts.append(both[:n] + both[n:])
    return jnp.concatenate(parts, axis=1)


def backward_spans(sizes, parity, cols_ref, live_ref, rows_ref, blocks_ref, spread):
    row_count, _, slots, width, bs = sizes
    per_span = rows_ref.shape[2] // bs
    me_col = lax.axis_index("col")
    me_row = lax.axis_index("row")

    def one_span(h, carry):
        own = split_rows(rows_ref[h, :width, :])
        for o in range(per_span):
            b = (me_row ^ (2 * h + parity)) * per_span + o
            tile = jnp.concatenate([blocks_ref[b, k] for k in range(slots)], axis=1)
            back = dot_nn(own[:, o * bs : (o + 1) * bs], tile, None)
            back = back[:width] + back[width:]
            for k in range(slots):
                at = place(cols_ref, b, k, me_col, per_span, row_count)
                w = (k < live_ref[0, b]).astype(f32)
                spread[at] += back[:, k * bs : (k + 1) * bs] * w
        return carry

    lax.fori_loop(0, row_count // 2, one_span, 0)


def back_even_kernel(sizes, cols_ref, live_ref, even_ref, blocks_ref, spread_ref):
    spread_ref[...] = jnp.zeros_like(spread_ref)
    backward_spans(sizes, 0, cols_ref, live_ref, even_ref, blocks_ref, spread_ref)


def back_odd_kernel(sizes, cols_ref, live_ref, odd_ref, blocks_ref, begun_ref, *rest):
    bs = sizes[4]
    out_refs, spread = rest[:-1], rest[-1]
    spread[...] = begun_ref[...]
    backward_spans(sizes, 1, cols_ref, live_ref, odd_ref, blocks_ref, spread)
    per_span = odd_ref.shape[2] // bs
    for s, out_ref in enumerate(out_refs):
        for o in range(per_span):
            out_ref[:, o * bs : (o + 1) * bs] = spread[s * per_span + o]


def put(ref, vectors, extra):
    h, n = vectors.shape[0] // 2, vectors.shape[1]
    ref[:, :n] = vectors[:h]
    ref[:, n : 2 * n] = vectors[h:]
    ref[:, 2 * n :] = extra


def take(message):
    n = (message.shape[1] - LANES) // 2
    return jnp.concatenate([message[:, :n], message[:, n : 2 * n]], axis=0), message[:, 2 * n :]


def fold_kernel(keep_ref, got_ref, extra_ref, got_extra_ref, low_ref, high_ref):
    extra = extra_ref[...] + got_extra_ref[...]
    n = low_ref.shape[0]
    for i, out_ref in enumerate((low_ref, high_ref)):
        for h in range(n):
            put(out_ref.at[h], keep_ref[i * n + h] + got_ref[i * n + h], extra)


def fold_more_kernel(keep_ref, got_ref, low_ref, high_ref):
    n = low_ref.shape[0]
    low_ref[...] = keep_ref[:n] + got_ref[:n]
    high_ref[...] = keep_ref[n:] + got_ref[n:]


def tree_sum(terms):
    while len(terms) > 1:
        terms = [terms[i] + terms[i + 1] for i in range(0, len(terms), 2)]
    return terms[0]


def middle_kernel(col_count, keep_ref, got_ref, *refs):
    back_refs = refs[:col_count]
    out_ref, y_ref = refs[col_count:]
    forward, sums = take(keep_ref[0] + got_ref[0])
    y = 0.5 * (forward + tree_sum([ref[...] for ref in back_refs]))
    y_ref[...] = y
    put(out_ref, y, sums)


def solve_kernel(col_count, width, *rest):
    y_refs = rest[:col_count]
    aux_ref, wide_ref = rest[col_count:]
    w = width
    sums = tree_sum([take(y_ref[...])[1] for y_ref in y_refs])
    gram_x, xp, pp, xbx = (unpack(sums, i) for i in range(4))
    cross_x = 0.5 * (xbx + xbx.T)
    done = eliminate(jnp.concatenate([gram_x, eye(w), cross_x, xp], axis=1), w)
    inverse_l, below_p = done[:, w : 2 * w], done[:, 3 * w : 4 * w]
    coefficient = dot_tn(inverse_l, done[:, 2 * w : 3 * w])
    xr = cross_x - dot_nn(gram_x, coefficient)
    aux_ref[...] = jnp.concatenate(
        [-coefficient.T, coefficient, xr, xp, pp, cross_x, inverse_l, jnp.zeros_like(xp)], axis=1
    )
    upper = jnp.concatenate([dot_nn(inverse_l, xr), below_p], axis=1)
    wide_ref[...] = jnp.concatenate(
        [dot_tn(upper, upper), -dot_tn(upper, inverse_l), jnp.zeros((2 * w, w), f32)], axis=1
    )


def forward_rest_kernel(sizes, cols_ref, live_ref, aux_ref, *rest):
    row_count, col_count, _, width, bs = sizes
    y_refs, x_refs = (rest[i * col_count : (i + 1) * col_count] for i in range(2))
    blocks_ref, out_ref, resid_ref, resid_out_ref, picks = rest[2 * col_count :]
    span_rows = out_ref.shape[2]
    per_span = span_rows // bs
    me_col = lax.axis_index("col")
    me_row = lax.axis_index("row")
    minus_c_t = aux_ref[:, :width]
    for s in range(col_count):
        rest_s = take(y_refs[s][...])[0] + dot_nn(minus_c_t, x_refs[s][:width])
        if s == 0:
            resid_ref[...] = rest_s
            resid_out_ref[...] = rest_s
        both = jnp.concatenate([rest_s, x_refs[s][width:]], axis=0)
        for o in range(per_span):
            picks[s * per_span + o] = split_rows(both[:, o * bs : (o + 1) * bs])

    def two_spans(h, carry):
        for s in (2 * h, 2 * h + 1):
            out_ref[s] = forward_span(
                sizes, s, cols_ref, live_ref, picks, blocks_ref, per_span, me_row, me_col
            )
        return carry

    lax.fori_loop(0, row_count // 2, two_spans, 0)


def iota(shape, axis):
    return lax.broadcasted_iota(jnp.int32, shape, axis)


def pack(matrices):
    h = matrices[0].shape[0] // 2
    return jnp.concatenate([part for m in matrices for part in (m[:h], m[h:])], axis=1)


def unpack(packed, i):
    w = 2 * packed.shape[0]
    at = 2 * i * w
    return jnp.concatenate([packed[:, at : at + w], packed[:, at + w : at + 2 * w]], axis=0)


def gram_kernel(
    width, half, aux_ref, even_ref, odd_ref, yeven_ref, yodd_ref, forward_ref, pair_ref,
    resid_ref, part_ref,
):
    w = width
    minus_c_t = aux_ref[:, :w]

    def two_spans(h, cross):
        for i, (rows_ref, y_ref) in enumerate(((even_ref, yeven_ref), (odd_ref, yodd_ref))):
            rest_q = y_ref[h] + three_pass(dot_nn, minus_c_t, rows_ref[h, :w, :])
            both = jnp.concatenate([rest_q, rows_ref[h, w:, :]], axis=0)
            cross = cross + three_pass(dot_nt, both, forward_ref[2 * h + i])
        return cross

    mine = resid_ref[...]
    gram = dot_nt(mine, jnp.concatenate([mine, pair_ref[w:]], axis=0))
    cross = lax.fori_loop(0, half, two_spans, jnp.zeros((2 * w, 2 * w), f32))
    rar, pap = cross[:w, :w], cross[w:, w:]
    rar = 0.5 * (rar + rar.T)
    pap = 0.5 * (pap + pap.T)
    rap = 0.5 * (cross[:w, w:] + cross[w:, :w].T)
    row, lane = iota((w, w), 0), iota((w, w), 1)
    diagonal = jnp.sum(jnp.where(row == lane, rar, 0.0), axis=1, keepdims=True)
    first = jnp.where(row <= lane, gram[:, :w], rar)
    corner = jnp.where((row == w - 1) & (lane == 1), diagonal[0:1, 0:1], 0.0)
    second = jnp.where(row <= lane, pap, jnp.where(lane == 0, diagonal, corner))
    part = pack([first, second, gram[:, w:], rap])
    for d in range(part_ref.shape[0]):
        part_ref[d] = part


def last_kernel(
    width, scale, parts_ref, aux_ref, wide_ref, xp_ref, resid_ref, x_next_ref, reduced_ref
):
    w = width
    total = parts_ref[0]
    for d in range(1, parts_ref.shape[0]):
        total = total + parts_ref[d]
    first, second, rp, rap = (unpack(total, i) for i in range(4))
    row, lane = iota((w, w), 0), iota((w, w), 1)
    below = first.T
    diagonal = jnp.where(iota((w, 1), 0) == 0, second[w - 1 : w, 1:2], second[:, 0:1])
    rr = jnp.where(row <= lane, first, below)
    rar = jnp.where(row > lane, first, jnp.where(row < lane, below, diagonal))
    pap = jnp.where(row <= lane, second, second.T)
    coefficient, xr, xp, pp, xax, inverse_x = (aux_ref[:, i * w : (i + 1) * w] for i in range(1, 7))
    schur = (
        jnp.concatenate(
            [jnp.concatenate([rr, rp], axis=1), jnp.concatenate([rp.T, pp], axis=1)], axis=0
        )
        - wide_ref[:, : 2 * w]
    )
    xar = rr + dot_tn(coefficient, xr)
    xap = rp + dot_tn(coefficient, xp)
    gram_apply = jnp.concatenate(
        [
            jnp.concatenate([xax, xar, xap], axis=1),
            jnp.concatenate([xar.T, rar, rap], axis=1),
            jnp.concatenate([xap.T, rap.T, pap], axis=1),
        ],
        axis=0,
    )
    n = 3 * w
    rest = eliminate(
        jnp.concatenate([schur, eye(2 * w), wide_ref[:, 2 * w : 3 * w]], axis=1), 2 * w
    )
    inverse_l = jnp.concatenate(
        [
            jnp.concatenate([inverse_x, jnp.zeros((w, 2 * w), f32)], axis=1),
            jnp.concatenate([rest[:, 4 * w : 5 * w], rest[:, 2 * w : 4 * w]], axis=1),
        ],
        axis=0,
    )
    reduced = dot_nt(dot_nn(inverse_l, gram_apply), inverse_l)
    reduced_ref[...] = reduced
    shifted = reduced + 3.0 * eye(n)
    target = dot_nn(shifted, shifted[:, :w])
    gram_fresh = dot_tn(target, target)
    mixing = dot_tn(target, inverse_l)
    weights = scale * eliminate(jnp.concatenate([gram_fresh, mixing], axis=1), w)[:, w:]
    basis = jnp.concatenate([xp_ref[:w, :], resid_ref[...], xp_ref[w:, :]], axis=0)
    x_next_ref[...] = dot_nn(weights, basis)


def per_device(block_vecs, direction, blocks, block_cols, live_counts):
    row_count = lax.axis_size("row")
    col_count = lax.axis_size("col")
    width, span_rows = block_vecs.shape
    block_rows, slots, bs = blocks.shape[:3]
    per_span = span_rows // bs
    half = row_count // 2
    order_total = span_rows * row_count * col_count
    col_blocks = col_count * per_span
    sizes = (row_count, col_count, slots, width, bs)
    shape = lambda *dims: jax.ShapeDtypeStruct(dims, f32)
    in_hbm = lambda array: pltpu.with_memory_space_constraint(array, HBM)
    spec = {
        "v": pl.BlockSpec(memory_space=VMEM),
        "s": pl.BlockSpec(memory_space=SMEM),
        "h": pl.BlockSpec(memory_space=HBM),
    }

    def call(kernel, ins, args, outs, scratch=(), cost=None):
        return pl.pallas_call(
            kernel,
            in_specs=[spec[letter] for letter in ins],
            out_specs=[spec["v"]] * len(outs),
            out_shape=outs,
            scratch_shapes=scratch,
            compiler_params=pltpu.CompilerParams(vmem_limit_bytes=VMEM_LIMIT),
            cost_estimate=cost,
        )(*args)

    def swap(array, axis, s):
        return lax.ppermute(array, axis, [(i, i ^ s) for i in range(lax.axis_size(axis))])

    far = list(reversed(range(1, col_count)))
    bits = row_bits(row_count)

    def gather_rows(array):
        even = array[None]
        for bit in bits:
            got = swap(even, "row", bit)
            even = jnp.concatenate([even, got], axis=0)
        return even, swap(even, "row", 1)

    def over_col(arrays):
        got = {s: swap(arrays[s], "col", s) for s in far}
        return [arrays[0]] + [got[s] for s in range(1, col_count)]

    pair, cols, live = call(
        load_kernel,
        "hhhh",
        [in_hbm(a) for a in (block_vecs, direction, block_cols.T, live_counts.T)],
        [
            shape(2 * width, span_rows),
            jax.ShapeDtypeStruct((slots, block_rows), jnp.int32),
            jax.ShapeDtypeStruct((1, block_rows), jnp.int32),
        ],
        [pltpu.SemaphoreType.DMA((4,))],
        pl.CostEstimate(flops=LOAD_FLOPS, bytes_accessed=0, transcendentals=0),
    )
    pair_cols = over_col([pair] * col_count)
    pair_even, pair_odd = gather_rows(pair)
    (begun,) = call(
        functools.partial(back_even_kernel, sizes),
        "ssvv",
        [cols, live, pair_even, blocks],
        [shape(col_blocks, width, bs)],
    )
    backs = call(
        functools.partial(back_odd_kernel, sizes),
        "ssvvv",
        [cols, live, pair_odd, blocks, begun],
        [shape(width, span_rows)] * col_count,
        [pltpu.VMEM((col_blocks, width, bs), f32)],
    )
    keep, send, extra = call(
        functools.partial(forward_kernel, sizes),
        "ssvv" + "v" * (col_count + 1),
        [cols, live, pair_even, pair_odd, *pair_cols, blocks],
        [shape(half, width, span_rows)] * 2 + [shape(width // 2, LANES)],
        [pltpu.VMEM((col_blocks, 2 * width, bs), bf16)],
    )
    got_pair = swap(send, "row", 1)
    got_extra = swap(extra, "row", 1)
    got_backs = over_col(backs)
    low, high = call(
        fold_kernel,
        "vvvv",
        [keep, got_pair, extra, got_extra],
        [shape(half // 2, width // 2, 2 * span_rows + LANES)] * 2,
    )
    for bit in reversed(bits):
        got = swap(high, "row", bit)
        if bit != bits[0]:
            low, high = call(
                fold_more_kernel,
                "vv",
                [low, got],
                [shape(low.shape[0] // 2, width // 2, 2 * span_rows + LANES)] * 2,
            )
    message, image = call(
        functools.partial(middle_kernel, col_count),
        "v" * (2 + col_count),
        [low, got, *got_backs],
        [shape(width // 2, 2 * span_rows + LANES), shape(width, span_rows)],
    )
    image_cols = over_col([message] * col_count)
    image_even, image_odd = gather_rows(image)
    aux, wide = call(
        functools.partial(solve_kernel, col_count, width),
        "v" * col_count,
        image_cols,
        [shape(width, LANES), shape(2 * width, 4 * width)],
    )
    forward_rp, resid, resid_out = call(
        functools.partial(forward_rest_kernel, sizes),
        "ssv" + "v" * (2 * col_count + 1),
        [cols, live, aux, *image_cols, *pair_cols, blocks],
        [shape(row_count, 2 * width, span_rows)] + [shape(width, span_rows)] * 2,
        [pltpu.VMEM((col_blocks, 4 * width, bs), bf16)],
    )
    (part,) = call(
        functools.partial(gram_kernel, width, half),
        "v" * 8,
        [aux, pair_even, pair_odd, image_even, image_odd, forward_rp, pair, resid],
        [shape(row_count * col_count, width // 2, LANES)],
    )
    parts = lax.all_to_all(part, ("col", "row"), 0, 0)
    x_next, reduced = call(
        functools.partial(last_kernel, width, math.sqrt(order_total)),
        "v" * 5,
        [parts, aux, wide, pair, resid],
        [shape(width, span_rows), shape(3 * width, 3 * width)],
    )
    return (x_next, reduced, resid_out)


def row_bits(row_count):
    return [1 << i for i in range(1, row_count.bit_length() - 1)]


def solution(mesh):
    return jax.shard_map(
        per_device,
        mesh=mesh,
        in_specs=(
            P(None, ("col", "row")),
            P(None, ("col", "row")),
            P("col", "row", None, None),
            P("col", "row"),
            P("col", "row"),
        ),
        out_specs=(P(None, ("col", "row")), P(), P(None, ("col", "row"))),
        check_vma=False,
    )
```

```python
import functools
import math

import jax
import jax.numpy as jnp
from jax import lax
from jax.experimental import pallas as pl
from jax.experimental.pallas import tpu as pltpu
from jax.sharding import PartitionSpec as P


highest = lax.Precision.HIGHEST
f32 = jnp.float32
bf16 = jnp.bfloat16
VMEM = pltpu.MemorySpace.VMEM
SMEM = pltpu.MemorySpace.SMEM
LANES = 128
VMEM_LIMIT = 16 * 1024 * 1024
LOAD_FLOPS = 20_000_000_000


def dot_nt(a, b, precision=highest):
    return lax.dot_general(
        a, b, (((1,), (1,)), ((), ())), precision=precision, preferred_element_type=f32
    )


def dot_nn(a, b, precision=highest):
    return lax.dot_general(
        a, b, (((1,), (0,)), ((), ())), precision=precision, preferred_element_type=f32
    )


def dot_tn(a, b, precision=highest):
    return lax.dot_general(
        a, b, (((0,), (0,)), ((), ())), precision=precision, preferred_element_type=f32
    )


def split(x):
    hi = x.astype(bf16)
    lo = (x - hi.astype(f32)).astype(bf16)
    return hi, lo


def split_rows(x):
    hi, lo = split(x)
    return jnp.concatenate([hi, lo], axis=0)


def three_pass(dot, a, b):
    a_hi, a_lo = split(a)
    b_hi, b_lo = split(b)
    n = a.shape[0]
    top = dot(jnp.concatenate([a_hi, a_lo], axis=0), b_hi, None)
    return top[:n] + top[n:] + dot(a_hi, b_lo, None)


def four_pass(dot, a, b):
    b_hi, b_lo = split(b)
    n = a.shape[0]
    both = split_rows(a)
    top, low = dot(both, b_hi, None), dot(both, b_lo, None)
    return top[:n] + (top[n:] + low[:n] + low[n:])


def eye(n):
    return (
        lax.broadcasted_iota(jnp.int32, (n, n), 0) == lax.broadcasted_iota(jnp.int32, (n, n), 1)
    ).astype(f32)


def eliminate(stack, n):
    m = stack.shape[1]
    row_at = lax.broadcasted_iota(jnp.int32, (n, m), 0)
    lane_at = lax.broadcasted_iota(jnp.int32, (n, m), 1)
    for j in range(0, n - 2, 2):
        one = jnp.broadcast_to(stack[:, j : j + 1], (n, m))
        two = jnp.broadcast_to(stack[:, j + 1 : j + 2], (n, m))
        a, b, d = one[j : j + 1], two[j : j + 1], two[j + 1 : j + 2]
        row_one, row_two = stack[j : j + 1], stack[j + 1 : j + 2]
        over = 1.0 / (a * d - b * b)
        scaled_one = (d * row_one - b * row_two) * over
        scaled_two = (a * row_two - b * row_one) * over
        below = row_at > j + 1
        stack = (
            stack
            - jnp.where(below, one, 0.0) * scaled_one
            - jnp.where(below, two, 0.0) * scaled_two
        )
    odd = row_at % 2 == 1
    above = jnp.concatenate([stack[n - 1 :], stack[: n - 1]], axis=0)
    pivot = jnp.sum(jnp.where(row_at == lane_at + 1, above, 0.0), axis=1, keepdims=True)
    beside = jnp.sum(jnp.where(row_at == lane_at + 1, stack, 0.0), axis=1, keepdims=True)
    ratio = beside / jnp.where(odd[:, :1], pivot, 1.0)
    stack = jnp.where(odd, stack - ratio * above, stack)
    diagonal = jnp.sum(jnp.where(row_at == lane_at, stack, 0.0), axis=1, keepdims=True)
    return stack / jnp.sqrt(diagonal)


def place(block_cols_ref, b, k, me_col, per_span, row_count):
    g = block_cols_ref[k, b]
    span = lax.div(g, per_span)
    return (lax.div(span, row_count) ^ me_col) * per_span + lax.rem(g, per_span)


def mark_kernel(mark_ref):
    mark_ref[...] = jnp.zeros_like(mark_ref)


def stack_kernel(*refs):
    out_ref, at = refs[-1], 0
    for ref in refs[:-2]:
        array = ref[...]
        n = array.shape[0] if array.ndim == 3 else 1
        out_ref[at : at + n] = array.reshape((n,) + array.shape[-2:])
        at += n


def forward_kernel(sizes, cols_ref, live_ref, even_ref, odd_ref, *rest):
    row_count, col_count, _, width, bs = sizes
    x_refs = rest[:col_count]
    p_ref, blocks_ref, keep_ref, send_ref, extra_ref, picks = rest[col_count:]
    per_span = keep_ref.shape[2] // bs
    me_col = lax.axis_index("col")
    me_row = lax.axis_index("row")
    for s in range(col_count):
        for o in range(per_span):
            picks[s * per_span + o] = split_rows(x_refs[s][:, o * bs : (o + 1) * bs])
    pair = jnp.concatenate([x_refs[0][...], p_ref[...]], axis=0)
    gram = four_pass(dot_nt, pair, pair)

    def two_spans(h, cross):
        for i, (out_ref, rows_ref) in enumerate(((keep_ref, even_ref), (send_ref, odd_ref))):
            forward = forward_span(
                sizes, 2 * h + i, cols_ref, live_ref, picks, blocks_ref, per_span, me_row, me_col
            )
            out_ref[h] = forward
            cross = cross + three_pass(dot_nt, rows_ref[h], forward)
        return cross

    cross = lax.fori_loop(0, row_count // 2, two_spans, jnp.zeros((width, width), f32))
    extra_ref[...] = pack([gram[:width, :width], gram[:width, width:], gram[width:, width:], cross])


def forward_span(
    sizes, s, cols_ref, live_ref, picks, blocks_ref, per_span, me_row, me_col
):
    row_count, _, slots, _, _ = sizes
    n = picks.shape[1] // 2
    parts = []
    for o in range(per_span):
        b = (me_row ^ s) * per_span + o
        tiles, chosen = [], []
        for k in range(slots):
            w = (k < live_ref[0, b]).astype(f32)
            at = place(cols_ref, b, k, me_col, per_span, row_count)
            tiles.append(blocks_ref[b, k])
            chosen.append(picks[at] * w.astype(bf16))
        both = dot_nt(jnp.concatenate(chosen, axis=1), jnp.concatenate(tiles, axis=1), None)
        parts.append(both[:n] + both[n:])
    return jnp.concatenate(parts, axis=1)


def backward_spans(sizes, parity, cols_ref, live_ref, rows_ref, blocks_ref, spread):
    row_count, _, slots, width, bs = sizes
    per_span = rows_ref.shape[2] // bs
    me_col = lax.axis_index("col")
    me_row = lax.axis_index("row")

    def one_span(h, carry):
        own = split_rows(rows_ref[h])
        for o in range(per_span):
            b = (me_row ^ (2 * h + parity)) * per_span + o
            tile = jnp.concatenate([blocks_ref[b, k] for k in range(slots)], axis=1)
            back = dot_nn(own[:, o * bs : (o + 1) * bs], tile, None)
            back = back[:width] + back[width:]
            for k in range(slots):
                at = place(cols_ref, b, k, me_col, per_span, row_count)
                w = (k < live_ref[0, b]).astype(f32)
                spread[at] += back[:, k * bs : (k + 1) * bs] * w
        return carry

    lax.fori_loop(0, row_count // 2, one_span, 0)


def back_even_kernel(sizes, cols_ref, live_ref, even_ref, blocks_ref, spread_ref):
    spread_ref[...] = jnp.zeros_like(spread_ref)
    backward_spans(sizes, 0, cols_ref, live_ref, even_ref, blocks_ref, spread_ref)


def back_odd_kernel(sizes, cols_ref, live_ref, odd_ref, blocks_ref, begun_ref, p_ref, *rest):
    width, bs = sizes[3:]
    out_refs, spread = rest[:-1], rest[-1]
    spread[...] = begun_ref[...]
    backward_spans(sizes, 1, cols_ref, live_ref, odd_ref, blocks_ref, spread)
    per_span = odd_ref.shape[2] // bs
    for s, out_ref in enumerate(out_refs):
        for o in range(per_span):
            out_ref[:width, o * bs : (o + 1) * bs] = spread[s * per_span + o]
        out_ref[width:] = p_ref[...]


def put(ref, vectors, extra):
    h, n = vectors.shape[0] // 2, vectors.shape[1]
    ref[:, :n] = vectors[:h]
    ref[:, n : 2 * n] = vectors[h:]
    ref[:, 2 * n :] = extra


def take(message):
    n = (message.shape[1] - LANES) // 2
    return jnp.concatenate([message[:, :n], message[:, n : 2 * n]], axis=0), message[:, 2 * n :]


def fold_kernel(keep_ref, got_ref, extra_ref, got_extra_ref, low_ref, high_ref):
    extra = extra_ref[...] + got_extra_ref[...]
    n = low_ref.shape[0]
    for i, out_ref in enumerate((low_ref, high_ref)):
        for h in range(n):
            put(out_ref.at[h], keep_ref[i * n + h] + got_ref[i * n + h], extra)


def fold_more_kernel(keep_ref, got_ref, low_ref, high_ref):
    n = low_ref.shape[0]
    low_ref[...] = keep_ref[:n] + got_ref[:n]
    high_ref[...] = keep_ref[n:] + got_ref[n:]


def tree_sum(terms):
    while len(terms) > 1:
        terms = [terms[i] + terms[i + 1] for i in range(0, len(terms), 2)]
    return terms[0]


def middle_kernel(col_count, keep_ref, got_ref, *refs):
    back_refs = refs[:col_count]
    out_ref, y_ref = refs[col_count:]
    width = y_ref.shape[0] // 2
    forward, sums = take(keep_ref[0] + got_ref[0])
    y = 0.5 * (forward + tree_sum([ref[:width] for ref in back_refs]))
    y_ref[:width] = y
    y_ref[width:] = back_refs[0][width:]
    put(out_ref, y, sums)


def solve_kernel(col_count, width, *rest):
    y_refs = rest[:col_count]
    aux_ref, wide_ref = rest[col_count:]
    w = width
    sums = tree_sum([take(y_ref[...])[1] for y_ref in y_refs])
    gram_x, xp, pp, xbx = (unpack(sums, i) for i in range(4))
    cross_x = 0.5 * (xbx + xbx.T)
    done = eliminate(jnp.concatenate([gram_x, eye(w), cross_x, xp], axis=1), w)
    inverse_l, below_p = done[:, w : 2 * w], done[:, 3 * w : 4 * w]
    coefficient = dot_tn(inverse_l, done[:, 2 * w : 3 * w])
    xr = cross_x - dot_nn(gram_x, coefficient)
    aux_ref[...] = jnp.concatenate(
        [-coefficient.T, coefficient, xr, xp, pp, cross_x, inverse_l, jnp.zeros_like(xp)], axis=1
    )
    upper = jnp.concatenate([dot_nn(inverse_l, xr), below_p], axis=1)
    wide_ref[...] = jnp.concatenate(
        [dot_tn(upper, upper), -dot_tn(upper, inverse_l), jnp.zeros((2 * w, w), f32)], axis=1
    )


def forward_rest_kernel(sizes, cols_ref, live_ref, aux_ref, *rest):
    row_count, col_count, _, width, bs = sizes
    y_refs, x_refs, p_refs = (rest[i * col_count : (i + 1) * col_count] for i in range(3))
    blocks_ref, out_ref, resid_ref, resid_out_ref, picks = rest[3 * col_count :]
    span_rows = out_ref.shape[2]
    per_span = span_rows // bs
    me_col = lax.axis_index("col")
    me_row = lax.axis_index("row")
    minus_c_t = aux_ref[:, :width]
    for s in range(col_count):
        rest_s = take(y_refs[s][...])[0] + dot_nn(minus_c_t, x_refs[s][...])
        if s == 0:
            resid_ref[...] = rest_s
            resid_out_ref[...] = rest_s
        both = jnp.concatenate([rest_s, p_refs[s][width:]], axis=0)
        for o in range(per_span):
            picks[s * per_span + o] = split_rows(both[:, o * bs : (o + 1) * bs])

    def two_spans(h, carry):
        for s in (2 * h, 2 * h + 1):
            out_ref[s] = forward_span(
                sizes, s, cols_ref, live_ref, picks, blocks_ref, per_span, me_row, me_col
            )
        return carry

    lax.fori_loop(0, row_count // 2, two_spans, 0)


def iota(shape, axis):
    return lax.broadcasted_iota(jnp.int32, shape, axis)


def pack(matrices):
    h = matrices[0].shape[0] // 2
    return jnp.concatenate([part for m in matrices for part in (m[:h], m[h:])], axis=1)


def unpack(packed, i):
    w = 2 * packed.shape[0]
    at = 2 * i * w
    return jnp.concatenate([packed[:, at : at + w], packed[:, at + w : at + 2 * w]], axis=0)


def gram_spans(width, parity, aux_ref, x_ref, y_ref, forward_ref):
    w = width
    minus_c_t = aux_ref[:, :w]

    def two_spans(i, cross):
        for h in (2 * i, 2 * i + 1):
            rest_q = y_ref[h, :w, :] + three_pass(dot_nn, minus_c_t, x_ref[h])
            both = jnp.concatenate([rest_q, y_ref[h, w:, :]], axis=0)
            cross = cross + three_pass(dot_nt, both, forward_ref[2 * h + parity])
        return cross

    return lax.fori_loop(0, x_ref.shape[0] // 2, two_spans, jnp.zeros((2 * w, 2 * w), f32))


def gram_even_kernel(
    width, aux_ref, x_ref, y_ref, forward_ref, p_ref, resid_ref, cross_ref, gram_ref
):
    mine = resid_ref[...]
    gram_ref[...] = four_pass(dot_nt, mine, jnp.concatenate([mine, p_ref[...]], axis=0))
    cross_ref[...] = gram_spans(width, 0, aux_ref, x_ref, y_ref, forward_ref)


def gram_odd_kernel(width, aux_ref, x_ref, y_ref, forward_ref, cross_ref, gram_ref, part_ref):
    w = width
    gram = gram_ref[...]
    cross = cross_ref[...] + gram_spans(w, 1, aux_ref, x_ref, y_ref, forward_ref)
    rar, pap = cross[:w, :w], cross[w:, w:]
    rar = 0.5 * (rar + rar.T)
    pap = 0.5 * (pap + pap.T)
    rap = 0.5 * (cross[:w, w:] + cross[w:, :w].T)
    row, lane = iota((w, w), 0), iota((w, w), 1)
    diagonal = jnp.sum(jnp.where(row == lane, rar, 0.0), axis=1, keepdims=True)
    first = jnp.where(row <= lane, gram[:, :w], rar)
    corner = jnp.where((row == w - 1) & (lane == 1), diagonal[0:1, 0:1], 0.0)
    second = jnp.where(row <= lane, pap, jnp.where(lane == 0, diagonal, corner))
    part = pack([first, second, gram[:, w:], rap])
    for d in range(part_ref.shape[0]):
        part_ref[d] = part


def last_kernel(
    width, scale, parts_ref, aux_ref, wide_ref, x_ref, yp_ref, resid_ref, x_next_ref, reduced_ref
):
    w = width
    total = parts_ref[0]
    for d in range(1, parts_ref.shape[0]):
        total = total + parts_ref[d]
    first, second, rp, rap = (unpack(total, i) for i in range(4))
    row, lane = iota((w, w), 0), iota((w, w), 1)
    below = first.T
    diagonal = jnp.where(iota((w, 1), 0) == 0, second[w - 1 : w, 1:2], second[:, 0:1])
    rr = jnp.where(row <= lane, first, below)
    rar = jnp.where(row > lane, first, jnp.where(row < lane, below, diagonal))
    pap = jnp.where(row <= lane, second, second.T)
    coefficient, xr, xp, pp, xax, inverse_x = (aux_ref[:, i * w : (i + 1) * w] for i in range(1, 7))
    schur = (
        jnp.concatenate(
            [jnp.concatenate([rr, rp], axis=1), jnp.concatenate([rp.T, pp], axis=1)], axis=0
        )
        - wide_ref[:, : 2 * w]
    )
    xar = rr + dot_tn(coefficient, xr)
    xap = rp + dot_tn(coefficient, xp)
    gram_apply = jnp.concatenate(
        [
            jnp.concatenate([xax, xar, xap], axis=1),
            jnp.concatenate([xar.T, rar, rap], axis=1),
            jnp.concatenate([xap.T, rap.T, pap], axis=1),
        ],
        axis=0,
    )
    n = 3 * w
    rest = eliminate(
        jnp.concatenate([schur, eye(2 * w), wide_ref[:, 2 * w : 3 * w]], axis=1), 2 * w
    )
    inverse_l = jnp.concatenate(
        [
            jnp.concatenate([inverse_x, jnp.zeros((w, 2 * w), f32)], axis=1),
            jnp.concatenate([rest[:, 4 * w : 5 * w], rest[:, 2 * w : 4 * w]], axis=1),
        ],
        axis=0,
    )
    reduced = dot_nt(dot_nn(inverse_l, gram_apply), inverse_l)
    reduced_ref[...] = reduced
    shifted = reduced + 3.0 * eye(n)
    target = dot_nn(shifted, shifted[:, :w])
    gram_fresh = dot_tn(target, target)
    mixing = dot_tn(target, inverse_l)
    weights = scale * eliminate(jnp.concatenate([gram_fresh, mixing], axis=1), w)[:, w:]
    basis = jnp.concatenate([x_ref[0], resid_ref[...], yp_ref[w:, :]], axis=0)
    x_next_ref[...] = dot_nn(weights, basis)


def per_device(block_vecs, direction, blocks, block_cols, live_counts):
    row_count = lax.axis_size("row")
    col_count = lax.axis_size("col")
    width, span_rows = block_vecs.shape
    slots, bs = blocks.shape[1:3]
    per_span = span_rows // bs
    half = row_count // 2
    order_total = span_rows * row_count * col_count
    col_blocks = col_count * per_span
    sizes = (row_count, col_count, slots, width, bs)
    shape = lambda *dims: jax.ShapeDtypeStruct(dims, f32)
    spec = {
        "v": pl.BlockSpec(memory_space=VMEM),
        "s": pl.BlockSpec(memory_space=SMEM),
    }

    def call(kernel, ins, args, outs, scratch=(), cost=None):
        return pl.pallas_call(
            kernel,
            in_specs=[spec[letter] for letter in ins],
            out_specs=[spec["v"]] * len(outs),
            out_shape=outs,
            scratch_shapes=scratch,
            compiler_params=pltpu.CompilerParams(vmem_limit_bytes=VMEM_LIMIT),
            cost_estimate=cost,
        )(*args)

    def swap(array, axis, s):
        return lax.ppermute(array, axis, [(i, i ^ s) for i in range(lax.axis_size(axis))])

    far = list(reversed(range(1, col_count)))
    bits = row_bits(row_count)
    window = pl.CostEstimate(flops=LOAD_FLOPS, bytes_accessed=0, transcendentals=0)

    def gather_rows(array):
        even = array
        for bit in bits:
            got = swap(even, "row", bit)
            (even,) = call(stack_kernel, "vvv", [even, got, mark], [shape(bit, *array.shape)])
        return even, swap(even, "row", 1)

    def over_col(arrays):
        got = {s: swap(arrays[s], "col", s) for s in far}
        return [arrays[0]] + [got[s] for s in range(1, col_count)]

    (mark,) = call(mark_kernel, "", [], [shape(8, LANES)], cost=window)
    cols, live = block_cols.T, live_counts.T
    x_cols = over_col([block_vecs] * col_count)
    x_even, x_odd = gather_rows(block_vecs)
    (begun,) = call(
        functools.partial(back_even_kernel, sizes),
        "ssvv",
        [cols, live, x_even, blocks],
        [shape(col_blocks, width, bs)],
    )
    backs = call(
        functools.partial(back_odd_kernel, sizes),
        "ssvvvv",
        [cols, live, x_odd, blocks, begun, direction],
        [shape(2 * width, span_rows)] * col_count,
        [pltpu.VMEM((col_blocks, width, bs), f32)],
    )
    keep, send, extra = call(
        functools.partial(forward_kernel, sizes),
        "ssvv" + "v" * (col_count + 2),
        [cols, live, x_even, x_odd, *x_cols, direction, blocks],
        [shape(half, width, span_rows)] * 2 + [shape(width // 2, LANES)],
        [pltpu.VMEM((col_blocks, 2 * width, bs), bf16)],
    )
    got_pair = swap(send, "row", 1)
    got_extra = swap(extra, "row", 1)
    got_backs = over_col(backs)
    low, high = call(
        fold_kernel,
        "vvvv",
        [keep, got_pair, extra, got_extra],
        [shape(half // 2, width // 2, 2 * span_rows + LANES)] * 2,
    )
    for bit in reversed(bits):
        got = swap(high, "row", bit)
        if bit != bits[0]:
            low, high = call(
                fold_more_kernel,
                "vv",
                [low, got],
                [shape(low.shape[0] // 2, width // 2, 2 * span_rows + LANES)] * 2,
            )
    message, image = call(
        functools.partial(middle_kernel, col_count),
        "v" * (2 + col_count),
        [low, got, *got_backs],
        [shape(width // 2, 2 * span_rows + LANES), shape(2 * width, span_rows)],
    )
    image_cols = over_col([message] * col_count)
    image_even, image_odd = gather_rows(image)
    aux, wide = call(
        functools.partial(solve_kernel, col_count, width),
        "v" * col_count,
        image_cols,
        [shape(width, LANES), shape(2 * width, 4 * width)],
    )
    forward_rp, resid, resid_out = call(
        functools.partial(forward_rest_kernel, sizes),
        "ssv" + "v" * (3 * col_count + 1),
        [cols, live, aux, *image_cols, *x_cols, *got_backs, blocks],
        [shape(row_count, 2 * width, span_rows)] + [shape(width, span_rows)] * 2,
        [pltpu.VMEM((col_blocks, 4 * width, bs), bf16)],
    )
    cross, gram = call(
        functools.partial(gram_even_kernel, width),
        "v" * 6,
        [aux, x_even, image_even, forward_rp, direction, resid],
        [shape(2 * width, 2 * width), shape(width, 2 * width)],
    )
    (part,) = call(
        functools.partial(gram_odd_kernel, width),
        "v" * 6,
        [aux, x_odd, image_odd, forward_rp, cross, gram],
        [shape(row_count * col_count, width // 2, LANES)],
    )
    parts = lax.all_to_all(part, ("col", "row"), 0, 0)
    x_next, reduced = call(
        functools.partial(last_kernel, width, math.sqrt(order_total)),
        "v" * 6,
        [parts, aux, wide, x_even, image, resid],
        [shape(width, span_rows), shape(3 * width, 3 * width)],
    )
    return (x_next, reduced, resid_out)


def row_bits(row_count):
    return [1 << i for i in range(1, row_count.bit_length() - 1)]


def solution(mesh):
    return jax.shard_map(
        per_device,
        mesh=mesh,
        in_specs=(
            P(None, ("col", "row")),
            P(None, ("col", "row")),
            P("col", "row", None, None),
            P("col", "row"),
            P("col", "row"),
        ),
        out_specs=(P(None, ("col", "row")), P(), P(None, ("col", "row"))),
        check_vma=False,
    )
```

```python
import functools
import math

import jax
import jax.numpy as jnp
from jax import lax
from jax.experimental import pallas as pl
from jax.experimental.pallas import tpu as pltpu
from jax.sharding import PartitionSpec as P


highest = lax.Precision.HIGHEST
f32 = jnp.float32
bf16 = jnp.bfloat16
VMEM = pltpu.MemorySpace.VMEM
SMEM = pltpu.MemorySpace.SMEM
LANES = 128
VMEM_LIMIT = 16 * 1024 * 1024
UNROLL = 4
LOAD_FLOPS = 20_000_000_000


def dot_nt(a, b, precision=highest):
    return lax.dot_general(
        a, b, (((1,), (1,)), ((), ())), precision=precision, preferred_element_type=f32
    )


def dot_nn(a, b, precision=highest):
    return lax.dot_general(
        a, b, (((1,), (0,)), ((), ())), precision=precision, preferred_element_type=f32
    )


def dot_tn(a, b, precision=highest):
    return lax.dot_general(
        a, b, (((0,), (0,)), ((), ())), precision=precision, preferred_element_type=f32
    )


def split(x):
    hi = x.astype(bf16)
    lo = (x - hi.astype(f32)).astype(bf16)
    return hi, lo


def split_rows(x):
    hi, lo = split(x)
    return jnp.concatenate([hi, lo], axis=0)


def three_pass(dot, a, b):
    a_hi, a_lo = split(a)
    b_hi, b_lo = split(b)
    n = a.shape[0]
    top = dot(jnp.concatenate([a_hi, a_lo], axis=0), b_hi, None)
    return top[:n] + top[n:] + dot(a_hi, b_lo, None)


def four_pass(dot, a, b):
    b_hi, b_lo = split(b)
    n = a.shape[0]
    both = split_rows(a)
    top, low = dot(both, b_hi, None), dot(both, b_lo, None)
    return top[:n] + (top[n:] + low[:n] + low[n:])


def eye(n):
    return (
        lax.broadcasted_iota(jnp.int32, (n, n), 0) == lax.broadcasted_iota(jnp.int32, (n, n), 1)
    ).astype(f32)


def eliminate(stack, n):
    m = stack.shape[1]
    row_at = lax.broadcasted_iota(jnp.int32, (n, m), 0)
    lane_at = lax.broadcasted_iota(jnp.int32, (n, m), 1)
    for j in range(0, n - 2, 2):
        one = jnp.broadcast_to(stack[:, j : j + 1], (n, m))
        two = jnp.broadcast_to(stack[:, j + 1 : j + 2], (n, m))
        a, b, d = one[j : j + 1], two[j : j + 1], two[j + 1 : j + 2]
        row_one, row_two = stack[j : j + 1], stack[j + 1 : j + 2]
        over = 1.0 / (a * d - b * b)
        scaled_one = (d * row_one - b * row_two) * over
        scaled_two = (a * row_two - b * row_one) * over
        below = row_at > j + 1
        stack = (
            stack
            - jnp.where(below, one, 0.0) * scaled_one
            - jnp.where(below, two, 0.0) * scaled_two
        )
    odd = row_at % 2 == 1
    above = jnp.concatenate([stack[n - 1 :], stack[: n - 1]], axis=0)
    pivot = jnp.sum(jnp.where(row_at == lane_at + 1, above, 0.0), axis=1, keepdims=True)
    beside = jnp.sum(jnp.where(row_at == lane_at + 1, stack, 0.0), axis=1, keepdims=True)
    ratio = beside / jnp.where(odd[:, :1], pivot, 1.0)
    stack = jnp.where(odd, stack - ratio * above, stack)
    diagonal = jnp.sum(jnp.where(row_at == lane_at, stack, 0.0), axis=1, keepdims=True)
    return stack / jnp.sqrt(diagonal)


def place(block_cols_ref, b, k, me_col, per_span, row_count):
    g = block_cols_ref[k, b]
    span = lax.div(g, per_span)
    return (lax.div(span, row_count) ^ me_col) * per_span + lax.rem(g, per_span)


def mark_kernel(mark_ref):
    mark_ref[...] = jnp.zeros_like(mark_ref)


def stack_kernel(*refs):
    out_ref, at = refs[-1], 0
    for ref in refs[:-2]:
        array = ref[...]
        n = array.shape[0] if array.ndim == 3 else 1
        out_ref[at : at + n] = array.reshape((n,) + array.shape[-2:])
        at += n


def forward_kernel(sizes, cols_ref, live_ref, even_ref, odd_ref, *rest):
    row_count, col_count, _, width, bs = sizes
    x_refs = rest[:col_count]
    p_ref, blocks_ref, keep_ref, send_ref, extra_ref, picks = rest[col_count:]
    per_span = keep_ref.shape[2] // bs
    me_col = lax.axis_index("col")
    me_row = lax.axis_index("row")
    for s in range(col_count):
        for o in range(per_span):
            picks[s * per_span + o] = split_rows(x_refs[s][:, o * bs : (o + 1) * bs])
    pair = jnp.concatenate([x_refs[0][...], p_ref[...]], axis=0)
    gram = four_pass(dot_nt, pair, pair)

    def two_spans(h, cross):
        for i, (out_ref, rows_ref) in enumerate(((keep_ref, even_ref), (send_ref, odd_ref))):
            forward = forward_span(
                sizes, 2 * h + i, cols_ref, live_ref, picks, blocks_ref, per_span, me_row, me_col
            )
            out_ref[h] = forward
            cross = cross + three_pass(dot_nt, rows_ref[h], forward)
        return cross

    cross = lax.fori_loop(
        0, row_count // 2, two_spans, jnp.zeros((width, width), f32), unroll=UNROLL
    )
    extra_ref[...] = pack([gram[:width, :width], gram[:width, width:], gram[width:, width:], cross])


def forward_span(
    sizes, s, cols_ref, live_ref, picks, blocks_ref, per_span, me_row, me_col
):
    row_count, _, slots, _, _ = sizes
    n = picks.shape[1] // 2
    parts = []
    for o in range(per_span):
        b = (me_row ^ s) * per_span + o
        tiles, chosen = [], []
        for k in range(slots):
            w = (k < live_ref[0, b]).astype(f32)
            at = place(cols_ref, b, k, me_col, per_span, row_count)
            tiles.append(blocks_ref[b, k])
            chosen.append(picks[at] * w.astype(bf16))
        both = dot_nt(jnp.concatenate(chosen, axis=1), jnp.concatenate(tiles, axis=1), None)
        parts.append(both[:n] + both[n:])
    return jnp.concatenate(parts, axis=1)


def backward_spans(sizes, parity, cols_ref, live_ref, rows_ref, blocks_ref, spread):
    row_count, _, slots, width, bs = sizes
    per_span = rows_ref.shape[2] // bs
    me_col = lax.axis_index("col")
    me_row = lax.axis_index("row")

    def one_span(h, carry):
        own = split_rows(rows_ref[h])
        for o in range(per_span):
            b = (me_row ^ (2 * h + parity)) * per_span + o
            tile = jnp.concatenate([blocks_ref[b, k] for k in range(slots)], axis=1)
            back = dot_nn(own[:, o * bs : (o + 1) * bs], tile, None)
            back = back[:width] + back[width:]
            for k in range(slots):
                at = place(cols_ref, b, k, me_col, per_span, row_count)
                w = (k < live_ref[0, b]).astype(f32)
                spread[at] += back[:, k * bs : (k + 1) * bs] * w
        return carry

    lax.fori_loop(0, row_count // 2, one_span, 0, unroll=UNROLL)


def back_even_kernel(sizes, cols_ref, live_ref, even_ref, blocks_ref, spread_ref):
    spread_ref[...] = jnp.zeros_like(spread_ref)
    backward_spans(sizes, 0, cols_ref, live_ref, even_ref, blocks_ref, spread_ref)


def back_odd_kernel(sizes, cols_ref, live_ref, odd_ref, blocks_ref, begun_ref, p_ref, *rest):
    width, bs = sizes[3:]
    out_refs, spread = rest[:-1], rest[-1]
    spread[...] = begun_ref[...]
    backward_spans(sizes, 1, cols_ref, live_ref, odd_ref, blocks_ref, spread)
    per_span = odd_ref.shape[2] // bs
    for s, out_ref in enumerate(out_refs):
        for o in range(per_span):
            out_ref[:width, o * bs : (o + 1) * bs] = spread[s * per_span + o]
        out_ref[width:] = p_ref[...]


def put(ref, vectors, extra):
    h, n = vectors.shape[0] // 2, vectors.shape[1]
    ref[:, :n] = vectors[:h]
    ref[:, n : 2 * n] = vectors[h:]
    ref[:, 2 * n :] = extra


def take(message):
    n = (message.shape[1] - LANES) // 2
    return jnp.concatenate([message[:, :n], message[:, n : 2 * n]], axis=0), message[:, 2 * n :]


def fold_kernel(keep_ref, got_ref, extra_ref, got_extra_ref, low_ref, high_ref):
    extra = extra_ref[...] + got_extra_ref[...]
    n = low_ref.shape[0]
    for i, out_ref in enumerate((low_ref, high_ref)):
        for h in range(n):
            put(out_ref.at[h], keep_ref[i * n + h] + got_ref[i * n + h], extra)


def fold_more_kernel(keep_ref, got_ref, low_ref, high_ref):
    n = low_ref.shape[0]
    low_ref[...] = keep_ref[:n] + got_ref[:n]
    high_ref[...] = keep_ref[n:] + got_ref[n:]


def tree_sum(terms):
    while len(terms) > 1:
        terms = [terms[i] + terms[i + 1] for i in range(0, len(terms), 2)]
    return terms[0]


def middle_kernel(col_count, keep_ref, got_ref, *refs):
    back_refs = refs[:col_count]
    out_ref, y_ref = refs[col_count:]
    width = y_ref.shape[0] // 2
    forward, sums = take(keep_ref[0] + got_ref[0])
    y = 0.5 * (forward + tree_sum([ref[:width] for ref in back_refs]))
    y_ref[:width] = y
    y_ref[width:] = back_refs[0][width:]
    put(out_ref, y, sums)


def solve_kernel(col_count, width, *rest):
    y_refs = rest[:col_count]
    (aux_ref,) = rest[col_count:]
    w = width
    sums = tree_sum([take(y_ref[...])[1] for y_ref in y_refs])
    gram_x, xp, pp, xbx = (unpack(sums, i) for i in range(4))
    cross_x = 0.5 * (xbx + xbx.T)
    done = eliminate(jnp.concatenate([gram_x, eye(w), cross_x, xp], axis=1), w)
    inverse_l, below_p = done[:, w : 2 * w], done[:, 3 * w : 4 * w]
    coefficient = dot_tn(inverse_l, done[:, 2 * w : 3 * w])
    aux_ref[...] = jnp.concatenate(
        [-coefficient.T, coefficient, below_p, xp, pp, cross_x, inverse_l, gram_x], axis=1
    )


def forward_rest_kernel(sizes, cols_ref, live_ref, aux_ref, *rest):
    row_count, col_count, _, width, bs = sizes
    y_refs, x_refs, p_refs = (rest[i * col_count : (i + 1) * col_count] for i in range(3))
    blocks_ref, out_ref, resid_ref, resid_out_ref, picks = rest[3 * col_count :]
    span_rows = out_ref.shape[2]
    per_span = span_rows // bs
    me_col = lax.axis_index("col")
    me_row = lax.axis_index("row")
    minus_c_t = aux_ref[:, :width]
    for s in range(col_count):
        rest_s = take(y_refs[s][...])[0] + dot_nn(minus_c_t, x_refs[s][...])
        if s == 0:
            resid_ref[...] = rest_s
            resid_out_ref[...] = rest_s
        both = jnp.concatenate([rest_s, p_refs[s][width:]], axis=0)
        for o in range(per_span):
            picks[s * per_span + o] = split_rows(both[:, o * bs : (o + 1) * bs])

    def two_spans(h, carry):
        for s in (2 * h, 2 * h + 1):
            out_ref[s] = forward_span(
                sizes, s, cols_ref, live_ref, picks, blocks_ref, per_span, me_row, me_col
            )
        return carry

    lax.fori_loop(0, row_count // 2, two_spans, 0, unroll=UNROLL)


def iota(shape, axis):
    return lax.broadcasted_iota(jnp.int32, shape, axis)


def pack(matrices):
    h = matrices[0].shape[0] // 2
    return jnp.concatenate([part for m in matrices for part in (m[:h], m[h:])], axis=1)


def unpack(packed, i):
    w = 2 * packed.shape[0]
    at = 2 * i * w
    return jnp.concatenate([packed[:, at : at + w], packed[:, at + w : at + 2 * w]], axis=0)


def gram_spans(width, parity, aux_ref, x_ref, y_ref, forward_ref):
    w = width
    minus_c_t = aux_ref[:, :w]

    def two_spans(i, cross):
        for h in (2 * i, 2 * i + 1):
            rest_q = y_ref[h, :w, :] + three_pass(dot_nn, minus_c_t, x_ref[h])
            both = jnp.concatenate([rest_q, y_ref[h, w:, :]], axis=0)
            cross = cross + three_pass(dot_nt, both, forward_ref[2 * h + parity])
        return cross

    zero = jnp.zeros((2 * w, 2 * w), f32)
    return lax.fori_loop(0, x_ref.shape[0] // 2, two_spans, zero, unroll=UNROLL // 2)


def gram_even_kernel(
    width, aux_ref, x_ref, y_ref, forward_ref, p_ref, resid_ref, cross_ref, gram_ref, wide_ref
):
    w = width
    coefficient, below_p, cross_x, inverse_l, gram_x = (
        aux_ref[:, i * w : (i + 1) * w] for i in (1, 2, 5, 6, 7)
    )
    xr = cross_x - dot_nn(gram_x, coefficient)
    upper = jnp.concatenate([dot_nn(inverse_l, xr), below_p], axis=1)
    wide_ref[...] = jnp.concatenate(
        [
            dot_tn(upper, upper),
            -dot_tn(upper, inverse_l),
            jnp.concatenate([xr, jnp.zeros((w, w), f32)], axis=0),
        ],
        axis=1,
    )
    mine = resid_ref[...]
    gram_ref[...] = four_pass(dot_nt, mine, jnp.concatenate([mine, p_ref[...]], axis=0))
    cross_ref[...] = gram_spans(width, 0, aux_ref, x_ref, y_ref, forward_ref)


def gram_odd_kernel(width, aux_ref, x_ref, y_ref, forward_ref, cross_ref, gram_ref, part_ref):
    w = width
    gram = gram_ref[...]
    cross = cross_ref[...] + gram_spans(w, 1, aux_ref, x_ref, y_ref, forward_ref)
    rar, pap = cross[:w, :w], cross[w:, w:]
    rar = 0.5 * (rar + rar.T)
    pap = 0.5 * (pap + pap.T)
    rap = 0.5 * (cross[:w, w:] + cross[w:, :w].T)
    row, lane = iota((w, w), 0), iota((w, w), 1)
    diagonal = jnp.sum(jnp.where(row == lane, rar, 0.0), axis=1, keepdims=True)
    first = jnp.where(row <= lane, gram[:, :w], rar)
    corner = jnp.where((row == w - 1) & (lane == 1), diagonal[0:1, 0:1], 0.0)
    second = jnp.where(row <= lane, pap, jnp.where(lane == 0, diagonal, corner))
    part = pack([first, second, gram[:, w:], rap])
    for d in range(part_ref.shape[0]):
        part_ref[d] = part


def last_kernel(
    width, scale, parts_ref, aux_ref, wide_ref, x_ref, yp_ref, resid_ref, x_next_ref, reduced_ref
):
    w = width
    total = parts_ref[0]
    for d in range(1, parts_ref.shape[0]):
        total = total + parts_ref[d]
    first, second, rp, rap = (unpack(total, i) for i in range(4))
    row, lane = iota((w, w), 0), iota((w, w), 1)
    below = first.T
    diagonal = jnp.where(iota((w, 1), 0) == 0, second[w - 1 : w, 1:2], second[:, 0:1])
    rr = jnp.where(row <= lane, first, below)
    rar = jnp.where(row > lane, first, jnp.where(row < lane, below, diagonal))
    pap = jnp.where(row <= lane, second, second.T)
    coefficient, xp, pp, xax, inverse_x = (
        aux_ref[:, i * w : (i + 1) * w] for i in (1, 3, 4, 5, 6)
    )
    xr = wide_ref[:w, 3 * w : 4 * w]
    schur = (
        jnp.concatenate(
            [jnp.concatenate([rr, rp], axis=1), jnp.concatenate([rp.T, pp], axis=1)], axis=0
        )
        - wide_ref[:, : 2 * w]
    )
    xar = rr + dot_tn(coefficient, xr)
    xap = rp + dot_tn(coefficient, xp)
    gram_apply = jnp.concatenate(
        [
            jnp.concatenate([xax, xar, xap], axis=1),
            jnp.concatenate([xar.T, rar, rap], axis=1),
            jnp.concatenate([xap.T, rap.T, pap], axis=1),
        ],
        axis=0,
    )
    n = 3 * w
    rest = eliminate(
        jnp.concatenate([schur, eye(2 * w), wide_ref[:, 2 * w : 3 * w]], axis=1), 2 * w
    )
    inverse_l = jnp.concatenate(
        [
            jnp.concatenate([inverse_x, jnp.zeros((w, 2 * w), f32)], axis=1),
            jnp.concatenate([rest[:, 4 * w : 5 * w], rest[:, 2 * w : 4 * w]], axis=1),
        ],
        axis=0,
    )
    reduced = dot_nt(dot_nn(inverse_l, gram_apply), inverse_l)
    reduced_ref[...] = reduced
    shifted = reduced + 3.0 * eye(n)
    target = dot_nn(shifted, shifted[:, :w])
    gram_fresh = dot_tn(target, target)
    mixing = dot_tn(target, inverse_l)
    weights = scale * eliminate(jnp.concatenate([gram_fresh, mixing], axis=1), w)[:, w:]
    basis = jnp.concatenate([x_ref[0], resid_ref[...], yp_ref[w:, :]], axis=0)
    x_next_ref[...] = dot_nn(weights, basis)


def per_device(block_vecs, direction, blocks, block_cols, live_counts):
    row_count = lax.axis_size("row")
    col_count = lax.axis_size("col")
    width, span_rows = block_vecs.shape
    slots, bs = blocks.shape[1:3]
    per_span = span_rows // bs
    half = row_count // 2
    order_total = span_rows * row_count * col_count
    col_blocks = col_count * per_span
    sizes = (row_count, col_count, slots, width, bs)
    shape = lambda *dims: jax.ShapeDtypeStruct(dims, f32)
    spec = {
        "v": pl.BlockSpec(memory_space=VMEM),
        "s": pl.BlockSpec(memory_space=SMEM),
    }

    def call(kernel, ins, args, outs, scratch=(), cost=None):
        return pl.pallas_call(
            kernel,
            in_specs=[spec[letter] for letter in ins],
            out_specs=[spec["v"]] * len(outs),
            out_shape=outs,
            scratch_shapes=scratch,
            compiler_params=pltpu.CompilerParams(vmem_limit_bytes=VMEM_LIMIT),
            cost_estimate=cost,
        )(*args)

    def swap(array, axis, s):
        return lax.ppermute(array, axis, [(i, i ^ s) for i in range(lax.axis_size(axis))])

    far = list(reversed(range(1, col_count)))
    bits = row_bits(row_count)
    window = pl.CostEstimate(flops=LOAD_FLOPS, bytes_accessed=0, transcendentals=0)

    def gather_rows(array):
        even = array
        for bit in bits:
            got = swap(even, "row", bit)
            (even,) = call(stack_kernel, "vvv", [even, got, mark], [shape(bit, *array.shape)])
        return even, swap(even, "row", 1)

    def over_col(arrays):
        got = {s: swap(arrays[s], "col", s) for s in far}
        return [arrays[0]] + [got[s] for s in range(1, col_count)]

    (mark,) = call(mark_kernel, "", [], [shape(8, LANES)], cost=window)
    cols, live = block_cols.T, live_counts.T
    x_cols = over_col([block_vecs] * col_count)
    x_even, x_odd = gather_rows(block_vecs)
    (begun,) = call(
        functools.partial(back_even_kernel, sizes),
        "ssvv",
        [cols, live, x_even, blocks],
        [shape(col_blocks, width, bs)],
    )
    backs = call(
        functools.partial(back_odd_kernel, sizes),
        "ssvvvv",
        [cols, live, x_odd, blocks, begun, direction],
        [shape(2 * width, span_rows)] * col_count,
        [pltpu.VMEM((col_blocks, width, bs), f32)],
    )
    keep, send, extra = call(
        functools.partial(forward_kernel, sizes),
        "ssvv" + "v" * (col_count + 2),
        [cols, live, x_even, x_odd, *x_cols, direction, blocks],
        [shape(half, width, span_rows)] * 2 + [shape(width // 2, LANES)],
        [pltpu.VMEM((col_blocks, 2 * width, bs), bf16)],
    )
    got_pair = swap(send, "row", 1)
    got_extra = swap(extra, "row", 1)
    got_backs = over_col(backs)
    low, high = call(
        fold_kernel,
        "vvvv",
        [keep, got_pair, extra, got_extra],
        [shape(half // 2, width // 2, 2 * span_rows + LANES)] * 2,
    )
    for bit in reversed(bits):
        got = swap(high, "row", bit)
        if bit != bits[0]:
            low, high = call(
                fold_more_kernel,
                "vv",
                [low, got],
                [shape(low.shape[0] // 2, width // 2, 2 * span_rows + LANES)] * 2,
            )
    message, image = call(
        functools.partial(middle_kernel, col_count),
        "v" * (2 + col_count),
        [low, got, *got_backs],
        [shape(width // 2, 2 * span_rows + LANES), shape(2 * width, span_rows)],
    )
    image_cols = over_col([message] * col_count)
    image_even, image_odd = gather_rows(image)
    (aux,) = call(
        functools.partial(solve_kernel, col_count, width),
        "v" * col_count,
        image_cols,
        [shape(width, 8 * width)],
    )
    forward_rp, resid, resid_out = call(
        functools.partial(forward_rest_kernel, sizes),
        "ssv" + "v" * (3 * col_count + 1),
        [cols, live, aux, *image_cols, *x_cols, *got_backs, blocks],
        [shape(row_count, 2 * width, span_rows)] + [shape(width, span_rows)] * 2,
        [pltpu.VMEM((col_blocks, 4 * width, bs), bf16)],
    )
    cross, gram, wide = call(
        functools.partial(gram_even_kernel, width),
        "v" * 6,
        [aux, x_even, image_even, forward_rp, direction, resid],
        [shape(2 * width, 2 * width), shape(width, 2 * width), shape(2 * width, 4 * width)],
    )
    (part,) = call(
        functools.partial(gram_odd_kernel, width),
        "v" * 6,
        [aux, x_odd, image_odd, forward_rp, cross, gram],
        [shape(row_count * col_count, width // 2, LANES)],
    )
    parts = lax.all_to_all(part, ("col", "row"), 0, 0)
    x_next, reduced = call(
        functools.partial(last_kernel, width, math.sqrt(order_total)),
        "v" * 6,
        [parts, aux, wide, x_even, image, resid],
        [shape(width, span_rows), shape(3 * width, 3 * width)],
    )
    return (x_next, reduced, resid_out)


def row_bits(row_count):
    return [1 << i for i in range(1, row_count.bit_length() - 1)]


def solution(mesh):
    return jax.shard_map(
        per_device,
        mesh=mesh,
        in_specs=(
            P(None, ("col", "row")),
            P(None, ("col", "row")),
            P("col", "row", None, None),
            P("col", "row"),
            P("col", "row"),
        ),
        out_specs=(P(None, ("col", "row")), P(), P(None, ("col", "row"))),
        check_vma=False,
    )
```

```python
import functools
import math

import jax
import jax.numpy as jnp
from jax import lax
from jax.experimental import pallas as pl
from jax.experimental.pallas import tpu as pltpu
from jax.sharding import PartitionSpec as P


highest = lax.Precision.HIGHEST
f32 = jnp.float32
bf16 = jnp.bfloat16
VMEM = pltpu.MemorySpace.VMEM
SMEM = pltpu.MemorySpace.SMEM
LANES = 128
VMEM_LIMIT = 16 * 1024 * 1024
UNROLL = 4
LOAD_FLOPS = 20_000_000_000


def dot_nt(a, b, precision=highest):
    return lax.dot_general(
        a, b, (((1,), (1,)), ((), ())), precision=precision, preferred_element_type=f32
    )


def dot_nn(a, b, precision=highest):
    return lax.dot_general(
        a, b, (((1,), (0,)), ((), ())), precision=precision, preferred_element_type=f32
    )


def dot_tn(a, b, precision=highest):
    return lax.dot_general(
        a, b, (((0,), (0,)), ((), ())), precision=precision, preferred_element_type=f32
    )


def split(x):
    hi = x.astype(bf16)
    lo = (x - hi.astype(f32)).astype(bf16)
    return hi, lo


def split_rows(x):
    hi, lo = split(x)
    return jnp.concatenate([hi, lo], axis=0)


def three_pass(dot, a, b):
    a_hi, a_lo = split(a)
    b_hi, b_lo = split(b)
    n = a.shape[0]
    top = dot(jnp.concatenate([a_hi, a_lo], axis=0), b_hi, None)
    return top[:n] + top[n:] + dot(a_hi, b_lo, None)


def four_pass(dot, a, b):
    b_hi, b_lo = split(b)
    n = a.shape[0]
    both = split_rows(a)
    top, low = dot(both, b_hi, None), dot(both, b_lo, None)
    return top[:n] + (top[n:] + low[:n] + low[n:])


def eye(n):
    return (
        lax.broadcasted_iota(jnp.int32, (n, n), 0) == lax.broadcasted_iota(jnp.int32, (n, n), 1)
    ).astype(f32)


def eliminate(stack, n):
    m = stack.shape[1]
    row_at = lax.broadcasted_iota(jnp.int32, (n, m), 0)
    lane_at = lax.broadcasted_iota(jnp.int32, (n, m), 1)
    for j in range(0, n - 2, 2):
        one = jnp.broadcast_to(stack[:, j : j + 1], (n, m))
        two = jnp.broadcast_to(stack[:, j + 1 : j + 2], (n, m))
        a, b, d = one[j : j + 1], two[j : j + 1], two[j + 1 : j + 2]
        row_one, row_two = stack[j : j + 1], stack[j + 1 : j + 2]
        over = 1.0 / (a * d - b * b)
        scaled_one = (d * row_one - b * row_two) * over
        scaled_two = (a * row_two - b * row_one) * over
        below = row_at > j + 1
        stack = (
            stack
            - jnp.where(below, one, 0.0) * scaled_one
            - jnp.where(below, two, 0.0) * scaled_two
        )
    odd = row_at % 2 == 1
    above = jnp.concatenate([stack[n - 1 :], stack[: n - 1]], axis=0)
    pivot = jnp.sum(jnp.where(row_at == lane_at + 1, above, 0.0), axis=1, keepdims=True)
    beside = jnp.sum(jnp.where(row_at == lane_at + 1, stack, 0.0), axis=1, keepdims=True)
    ratio = beside / jnp.where(odd[:, :1], pivot, 1.0)
    stack = jnp.where(odd, stack - ratio * above, stack)
    diagonal = jnp.sum(jnp.where(row_at == lane_at, stack, 0.0), axis=1, keepdims=True)
    return stack / jnp.sqrt(diagonal)


def table_kernel(cols_ref, live_ref, table_ref):
    slot = lax.broadcasted_iota(jnp.int32, cols_ref.shape, 0)
    table_ref[...] = 2 * cols_ref[...] + (slot < live_ref[...]).astype(jnp.int32)


def place(table_ref, b, k, me_col, per_span, row_count):
    g = lax.shift_right_logical(table_ref[k, b], 1)
    span = lax.div(g, per_span)
    return (lax.div(span, row_count) ^ me_col) * per_span + lax.rem(g, per_span)


def mark_kernel(mark_ref):
    mark_ref[...] = jnp.zeros_like(mark_ref)


def stack_kernel(*refs):
    out_ref, at = refs[-1], 0
    for ref in refs[:-2]:
        array = ref[...]
        n = array.shape[0] if array.ndim == 3 else 1
        out_ref[at : at + n] = array.reshape((n,) + array.shape[-2:])
        at += n


def forward_kernel(sizes, table_ref, even_ref, odd_ref, *rest):
    row_count, col_count, _, width, bs = sizes
    x_refs = rest[:col_count]
    gram_ref, blocks_ref, begun_ref, p_ref, keep_ref, send_ref, extra_ref = rest[
        col_count : col_count + 7
    ]
    back_refs, picks, spread = rest[col_count + 7 : -2], rest[-2], rest[-1]
    per_span = keep_ref.shape[2] // bs
    me_col = lax.axis_index("col")
    me_row = lax.axis_index("row")
    for s in range(col_count):
        for o in range(per_span):
            picks[s * per_span + o] = split_rows(x_refs[s][:, o * bs : (o + 1) * bs])
    gram = gram_ref[...]
    spread[...] = begun_ref[...]
    n = odd_ref.shape[0]
    backward_spans(sizes, 1, table_ref, odd_ref, blocks_ref, spread, 0, n)
    for s, back_ref in enumerate(back_refs):
        for o in range(per_span):
            back_ref[:width, o * bs : (o + 1) * bs] = spread[s * per_span + o]
        back_ref[width:] = p_ref[...]

    def two_spans(h, cross):
        for i, (out_ref, rows_ref) in enumerate(((keep_ref, even_ref), (send_ref, odd_ref))):
            forward = forward_span(
                sizes, 2 * h + i, table_ref, picks, blocks_ref, per_span, me_row, me_col
            )
            out_ref[h] = forward
            cross = cross + three_pass(dot_nt, rows_ref[h], forward)
        return cross

    cross = lax.fori_loop(
        0, row_count // 2, two_spans, jnp.zeros((width, width), f32), unroll=UNROLL
    )
    extra_ref[...] = pack([gram[:width, :width], gram[:width, width:], gram[width:, width:], cross])


def forward_span(
    sizes, s, table_ref, picks, blocks_ref, per_span, me_row, me_col
):
    row_count, _, slots, _, _ = sizes
    n = picks.shape[1] // 2
    parts = []
    for o in range(per_span):
        b = (me_row ^ s) * per_span + o
        tiles, chosen = [], []
        for k in range(slots):
            w = (table_ref[k, b] & 1).astype(f32)
            at = place(table_ref, b, k, me_col, per_span, row_count)
            tiles.append(blocks_ref[b, k])
            chosen.append(picks[at] * w.astype(bf16))
        both = dot_nt(jnp.concatenate(chosen, axis=1), jnp.concatenate(tiles, axis=1), None)
        parts.append(both[:n] + both[n:])
    return jnp.concatenate(parts, axis=1)


def backward_spans(sizes, parity, table_ref, rows_ref, blocks_ref, spread, begin, end):
    row_count, _, slots, width, bs = sizes
    per_span = rows_ref.shape[2] // bs
    me_col = lax.axis_index("col")
    me_row = lax.axis_index("row")

    def one_span(h, carry):
        own = split_rows(rows_ref[h])
        for o in range(per_span):
            b = (me_row ^ (2 * h + parity)) * per_span + o
            tile = jnp.concatenate([blocks_ref[b, k] for k in range(slots)], axis=1)
            back = dot_nn(own[:, o * bs : (o + 1) * bs], tile, None)
            back = back[:width] + back[width:]
            for k in range(slots):
                at = place(table_ref, b, k, me_col, per_span, row_count)
                w = (table_ref[k, b] & 1).astype(f32)
                spread[at] += back[:, k * bs : (k + 1) * bs] * w
        return carry

    lax.fori_loop(begin, end, one_span, 0, unroll=min(UNROLL, end - begin))


def back_near_kernel(
    sizes, table_ref, near_ref, blocks_ref, p_ref, spread_ref, gram_ref
):
    spread_ref[...] = jnp.zeros_like(spread_ref)
    pair = jnp.concatenate([near_ref[0], p_ref[...]], axis=0)
    gram_ref[...] = four_pass(dot_nt, pair, pair)
    n = near_ref.shape[0]
    backward_spans(sizes, 0, table_ref, near_ref, blocks_ref, spread_ref, 0, n)


def back_even_kernel(
    sizes, near, table_ref, even_ref, blocks_ref, begun_ref, spread_ref
):
    spread_ref[...] = begun_ref[...]
    n = even_ref.shape[0]
    backward_spans(sizes, 0, table_ref, even_ref, blocks_ref, spread_ref, near, n)


def put(ref, vectors, extra):
    h, n = vectors.shape[0] // 2, vectors.shape[1]
    ref[:, :n] = vectors[:h]
    ref[:, n : 2 * n] = vectors[h:]
    ref[:, 2 * n :] = extra


def take(message):
    n = (message.shape[1] - LANES) // 2
    return jnp.concatenate([message[:, :n], message[:, n : 2 * n]], axis=0), message[:, 2 * n :]


def fold_kernel(keep_ref, got_ref, extra_ref, got_extra_ref, low_ref, high_ref):
    extra = extra_ref[...] + got_extra_ref[...]
    n = low_ref.shape[0]
    for i, out_ref in enumerate((low_ref, high_ref)):
        for h in range(n):
            put(out_ref.at[h], keep_ref[i * n + h] + got_ref[i * n + h], extra)


def fold_more_kernel(keep_ref, got_ref, low_ref, high_ref):
    n = low_ref.shape[0]
    low_ref[...] = keep_ref[:n] + got_ref[:n]
    high_ref[...] = keep_ref[n:] + got_ref[n:]


def tree_sum(terms):
    while len(terms) > 1:
        terms = [terms[i] + terms[i + 1] for i in range(0, len(terms), 2)]
    return terms[0]


def middle_kernel(col_count, keep_ref, got_ref, *refs):
    back_refs = refs[:col_count]
    out_ref, y_ref = refs[col_count:]
    width = y_ref.shape[0] // 2
    forward, sums = take(keep_ref[0] + got_ref[0])
    y = 0.5 * (forward + tree_sum([ref[:width] for ref in back_refs]))
    y_ref[:width] = y
    y_ref[width:] = back_refs[0][width:]
    put(out_ref, y, sums)


def solve(y_refs, aux_ref, w):
    sums = tree_sum([take(y_ref[...])[1] for y_ref in y_refs])
    gram_x, xp, pp, xbx = (unpack(sums, i) for i in range(4))
    cross_x = 0.5 * (xbx + xbx.T)
    done = eliminate(jnp.concatenate([gram_x, eye(w), cross_x, xp], axis=1), w)
    inverse_l, below_p = done[:, w : 2 * w], done[:, 3 * w : 4 * w]
    coefficient = dot_tn(inverse_l, done[:, 2 * w : 3 * w])
    minus_c_t = -coefficient.T
    aux_ref[...] = jnp.concatenate(
        [minus_c_t, coefficient, below_p, xp, pp, cross_x, inverse_l, gram_x], axis=1
    )
    return minus_c_t


def forward_rest_kernel(sizes, table_ref, *rest):
    row_count, col_count, _, width, bs = sizes
    y_refs, x_refs, p_refs = (rest[i * col_count : (i + 1) * col_count] for i in range(3))
    blocks_ref, out_ref, resid_ref, resid_out_ref, aux_ref, picks = rest[3 * col_count :]
    span_rows = out_ref.shape[2]
    per_span = span_rows // bs
    me_col = lax.axis_index("col")
    me_row = lax.axis_index("row")
    minus_c_t = solve(y_refs, aux_ref, width)
    for s in range(col_count):
        rest_s = take(y_refs[s][...])[0] + dot_nn(minus_c_t, x_refs[s][...])
        if s == 0:
            resid_ref[...] = rest_s
            resid_out_ref[...] = rest_s
        both = jnp.concatenate([rest_s, p_refs[s][width:]], axis=0)
        for o in range(per_span):
            picks[s * per_span + o] = split_rows(both[:, o * bs : (o + 1) * bs])

    def two_spans(h, carry):
        for s in (2 * h, 2 * h + 1):
            out_ref[s] = forward_span(
                sizes, s, table_ref, picks, blocks_ref, per_span, me_row, me_col
            )
        return carry

    lax.fori_loop(0, row_count // 2, two_spans, 0, unroll=UNROLL)


def iota(shape, axis):
    return lax.broadcasted_iota(jnp.int32, shape, axis)


def pack(matrices):
    h = matrices[0].shape[0] // 2
    return jnp.concatenate([part for m in matrices for part in (m[:h], m[h:])], axis=1)


def unpack(packed, i):
    w = 2 * packed.shape[0]
    at = 2 * i * w
    return jnp.concatenate([packed[:, at : at + w], packed[:, at + w : at + 2 * w]], axis=0)


def gram_spans(width, parity, aux_ref, x_ref, y_ref, forward_ref):
    w = width
    minus_c_t = aux_ref[:, :w]

    def two_spans(i, cross):
        for h in (2 * i, 2 * i + 1):
            rest_q = y_ref[h, :w, :] + three_pass(dot_nn, minus_c_t, x_ref[h])
            both = jnp.concatenate([rest_q, y_ref[h, w:, :]], axis=0)
            cross = cross + three_pass(dot_nt, both, forward_ref[2 * h + parity])
        return cross

    zero = jnp.zeros((2 * w, 2 * w), f32)
    return lax.fori_loop(0, x_ref.shape[0] // 2, two_spans, zero, unroll=UNROLL // 2)


def gram_even_kernel(
    width, aux_ref, x_ref, y_ref, forward_ref, p_ref, resid_ref, cross_ref, gram_ref, wide_ref
):
    w = width
    coefficient, below_p, cross_x, inverse_l, gram_x = (
        aux_ref[:, i * w : (i + 1) * w] for i in (1, 2, 5, 6, 7)
    )
    xr = cross_x - dot_nn(gram_x, coefficient)
    upper = jnp.concatenate([dot_nn(inverse_l, xr), below_p], axis=1)
    wide_ref[...] = jnp.concatenate(
        [
            dot_tn(upper, upper),
            -dot_tn(upper, inverse_l),
            jnp.concatenate([xr, jnp.zeros((w, w), f32)], axis=0),
        ],
        axis=1,
    )
    mine = resid_ref[...]
    gram_ref[...] = four_pass(dot_nt, mine, jnp.concatenate([mine, p_ref[...]], axis=0))
    cross_ref[...] = gram_spans(width, 0, aux_ref, x_ref, y_ref, forward_ref)


def gram_odd_kernel(width, aux_ref, x_ref, y_ref, forward_ref, cross_ref, gram_ref, part_ref):
    w = width
    gram = gram_ref[...]
    cross = cross_ref[...] + gram_spans(w, 1, aux_ref, x_ref, y_ref, forward_ref)
    rar, pap = cross[:w, :w], cross[w:, w:]
    rar = 0.5 * (rar + rar.T)
    pap = 0.5 * (pap + pap.T)
    rap = 0.5 * (cross[:w, w:] + cross[w:, :w].T)
    row, lane = iota((w, w), 0), iota((w, w), 1)
    diagonal = jnp.sum(jnp.where(row == lane, rar, 0.0), axis=1, keepdims=True)
    first = jnp.where(row <= lane, gram[:, :w], rar)
    corner = jnp.where((row == w - 1) & (lane == 1), diagonal[0:1, 0:1], 0.0)
    second = jnp.where(row <= lane, pap, jnp.where(lane == 0, diagonal, corner))
    part = pack([first, second, gram[:, w:], rap])
    for d in range(part_ref.shape[0]):
        part_ref[d] = part


def last_kernel(
    width, scale, parts_ref, aux_ref, wide_ref, x_ref, yp_ref, resid_ref, x_next_ref, reduced_ref
):
    w = width
    total = parts_ref[0]
    for d in range(1, parts_ref.shape[0]):
        total = total + parts_ref[d]
    first, second, rp, rap = (unpack(total, i) for i in range(4))
    row, lane = iota((w, w), 0), iota((w, w), 1)
    below = first.T
    diagonal = jnp.where(iota((w, 1), 0) == 0, second[w - 1 : w, 1:2], second[:, 0:1])
    rr = jnp.where(row <= lane, first, below)
    rar = jnp.where(row > lane, first, jnp.where(row < lane, below, diagonal))
    pap = jnp.where(row <= lane, second, second.T)
    coefficient, xp, pp, xax, inverse_x = (
        aux_ref[:, i * w : (i + 1) * w] for i in (1, 3, 4, 5, 6)
    )
    xr = wide_ref[:w, 3 * w : 4 * w]
    schur = (
        jnp.concatenate(
            [jnp.concatenate([rr, rp], axis=1), jnp.concatenate([rp.T, pp], axis=1)], axis=0
        )
        - wide_ref[:, : 2 * w]
    )
    xar = rr + dot_tn(coefficient, xr)
    xap = rp + dot_tn(coefficient, xp)
    gram_apply = jnp.concatenate(
        [
            jnp.concatenate([xax, xar, xap], axis=1),
            jnp.concatenate([xar.T, rar, rap], axis=1),
            jnp.concatenate([xap.T, rap.T, pap], axis=1),
        ],
        axis=0,
    )
    n = 3 * w
    rest = eliminate(
        jnp.concatenate([schur, eye(2 * w), wide_ref[:, 2 * w : 3 * w]], axis=1), 2 * w
    )
    inverse_l = jnp.concatenate(
        [
            jnp.concatenate([inverse_x, jnp.zeros((w, 2 * w), f32)], axis=1),
            jnp.concatenate([rest[:, 4 * w : 5 * w], rest[:, 2 * w : 4 * w]], axis=1),
        ],
        axis=0,
    )
    reduced = dot_nt(dot_nn(inverse_l, gram_apply), inverse_l)
    reduced_ref[...] = reduced
    shifted = reduced + 3.0 * eye(n)
    target = dot_nn(shifted, shifted[:, :w])
    gram_fresh = dot_tn(target, target)
    mixing = dot_tn(target, inverse_l)
    weights = scale * eliminate(jnp.concatenate([gram_fresh, mixing], axis=1), w)[:, w:]
    basis = jnp.concatenate([x_ref[0], resid_ref[...], yp_ref[w:, :]], axis=0)
    x_next_ref[...] = dot_nn(weights, basis)


def per_device(block_vecs, direction, blocks, block_cols, live_counts):
    row_count = lax.axis_size("row")
    col_count = lax.axis_size("col")
    width, span_rows = block_vecs.shape
    slots, bs = blocks.shape[1:3]
    per_span = span_rows // bs
    half = row_count // 2
    order_total = span_rows * row_count * col_count
    col_blocks = col_count * per_span
    sizes = (row_count, col_count, slots, width, bs)
    shape = lambda *dims: jax.ShapeDtypeStruct(dims, f32)
    spec = {
        "v": pl.BlockSpec(memory_space=VMEM),
        "s": pl.BlockSpec(memory_space=SMEM),
    }

    def call(kernel, ins, args, outs, scratch=(), cost=None):
        return pl.pallas_call(
            kernel,
            in_specs=[spec[letter] for letter in ins],
            out_specs=[spec["v"]] * len(outs),
            out_shape=outs,
            scratch_shapes=scratch,
            compiler_params=pltpu.CompilerParams(vmem_limit_bytes=VMEM_LIMIT),
            cost_estimate=cost,
        )(*args)

    def swap(array, axis, s):
        return lax.ppermute(array, axis, [(i, i ^ s) for i in range(lax.axis_size(axis))])

    far = list(reversed(range(1, col_count)))
    bits = row_bits(row_count)
    window = pl.CostEstimate(flops=LOAD_FLOPS, bytes_accessed=0, transcendentals=0)

    def gather_rows(array):
        even = array
        for bit in bits:
            got = swap(even, "row", bit)
            (even,) = call(stack_kernel, "vvv", [even, got, mark], [shape(bit, *array.shape)])
            if bit == bits[0]:
                near = even
        return near, even, swap(even, "row", 1)

    def over_col(arrays):
        got = {s: swap(arrays[s], "col", s) for s in far}
        return [arrays[0]] + [got[s] for s in range(1, col_count)]

    (mark,) = call(mark_kernel, "", [], [shape(8, LANES)], cost=window)
    (table,) = call(
        table_kernel,
        "vv",
        [block_cols.T, live_counts.T],
        [jax.ShapeDtypeStruct(block_cols.T.shape, jnp.int32)],
    )
    x_cols = over_col([block_vecs] * col_count)
    x_near, x_even, x_odd = gather_rows(block_vecs)
    begun, gram = call(
        functools.partial(back_near_kernel, sizes),
        "svvv",
        [table, x_near, blocks, direction],
        [shape(col_blocks, width, bs), shape(2 * width, 2 * width)],
    )
    if half > x_near.shape[0]:
        (begun,) = call(
            functools.partial(back_even_kernel, sizes, x_near.shape[0]),
            "svvv",
            [table, x_even, blocks, begun],
            [shape(col_blocks, width, bs)],
        )
    keep, send, extra, *backs = call(
        functools.partial(forward_kernel, sizes),
        "svv" + "v" * (col_count + 4),
        [table, x_even, x_odd, *x_cols, gram, blocks, begun, direction],
        [shape(half, width, span_rows)] * 2
        + [shape(width // 2, LANES)]
        + [shape(2 * width, span_rows)] * col_count,
        [
            pltpu.VMEM((col_blocks, 2 * width, bs), bf16),
            pltpu.VMEM((col_blocks, width, bs), f32),
        ],
    )
    got_pair = swap(send, "row", 1)
    got_extra = swap(extra, "row", 1)
    got_backs = over_col(backs)
    low, high = call(
        fold_kernel,
        "vvvv",
        [keep, got_pair, extra, got_extra],
        [shape(half // 2, width // 2, 2 * span_rows + LANES)] * 2,
    )
    for bit in reversed(bits):
        got = swap(high, "row", bit)
        if bit != bits[0]:
            low, high = call(
                fold_more_kernel,
                "vv",
                [low, got],
                [shape(low.shape[0] // 2, width // 2, 2 * span_rows + LANES)] * 2,
            )
    message, image = call(
        functools.partial(middle_kernel, col_count),
        "v" * (2 + col_count),
        [low, got, *got_backs],
        [shape(width // 2, 2 * span_rows + LANES), shape(2 * width, span_rows)],
    )
    image_cols = over_col([message] * col_count)
    _, image_even, image_odd = gather_rows(image)
    forward_rp, resid, resid_out, aux = call(
        functools.partial(forward_rest_kernel, sizes),
        "s" + "v" * (3 * col_count + 1),
        [table, *image_cols, *x_cols, *got_backs, blocks],
        [shape(row_count, 2 * width, span_rows)]
        + [shape(width, span_rows)] * 2
        + [shape(width, 8 * width)],
        [pltpu.VMEM((col_blocks, 4 * width, bs), bf16)],
    )
    cross, gram, wide = call(
        functools.partial(gram_even_kernel, width),
        "v" * 6,
        [aux, x_even, image_even, forward_rp, direction, resid],
        [shape(2 * width, 2 * width), shape(width, 2 * width), shape(2 * width, 4 * width)],
    )
    (part,) = call(
        functools.partial(gram_odd_kernel, width),
        "v" * 6,
        [aux, x_odd, image_odd, forward_rp, cross, gram],
        [shape(row_count * col_count, width // 2, LANES)],
    )
    parts = lax.all_to_all(part, ("col", "row"), 0, 0)
    x_next, reduced = call(
        functools.partial(last_kernel, width, math.sqrt(order_total)),
        "v" * 6,
        [parts, aux, wide, x_even, image, resid],
        [shape(width, span_rows), shape(3 * width, 3 * width)],
    )
    return (x_next, reduced, resid_out)


def row_bits(row_count):
    return [1 << i for i in range(1, row_count.bit_length() - 1)]


def solution(mesh):
    return jax.shard_map(
        per_device,
        mesh=mesh,
        in_specs=(
            P(None, ("col", "row")),
            P(None, ("col", "row")),
            P("col", "row", None, None),
            P("col", "row"),
            P("col", "row"),
        ),
        out_specs=(P(None, ("col", "row")), P(), P(None, ("col", "row"))),
        check_vma=False,
    )
```

```python
import functools
import math

import jax
import jax.numpy as jnp
from jax import lax
from jax.experimental import pallas as pl
from jax.experimental.pallas import tpu as pltpu
from jax.sharding import PartitionSpec as P


highest = lax.Precision.HIGHEST
f32 = jnp.float32
bf16 = jnp.bfloat16
VMEM = pltpu.MemorySpace.VMEM
SMEM = pltpu.MemorySpace.SMEM
LANES = 128
VMEM_LIMIT = 16 * 1024 * 1024
UNROLL = 4
LOAD_FLOPS = 20_000_000_000


def dot_nt(a, b, precision=highest):
    return lax.dot_general(
        a, b, (((1,), (1,)), ((), ())), precision=precision, preferred_element_type=f32
    )


def dot_nn(a, b, precision=highest):
    return lax.dot_general(
        a, b, (((1,), (0,)), ((), ())), precision=precision, preferred_element_type=f32
    )


def dot_tn(a, b, precision=highest):
    return lax.dot_general(
        a, b, (((0,), (0,)), ((), ())), precision=precision, preferred_element_type=f32
    )


def split(x):
    hi = x.astype(bf16)
    lo = (x - hi.astype(f32)).astype(bf16)
    return hi, lo


def split_rows(x):
    hi, lo = split(x)
    return jnp.concatenate([hi, lo], axis=0)


def three_pass(dot, a, b):
    a_hi, a_lo = split(a)
    b_hi, b_lo = split(b)
    n = a.shape[0]
    top = dot(jnp.concatenate([a_hi, a_lo], axis=0), b_hi, None)
    return top[:n] + top[n:] + dot(a_hi, b_lo, None)


def four_pass(dot, a, b):
    b_hi, b_lo = split(b)
    n = a.shape[0]
    both = split_rows(a)
    top, low = dot(both, b_hi, None), dot(both, b_lo, None)
    return top[:n] + (top[n:] + low[:n] + low[n:])


def eye(n):
    return (
        lax.broadcasted_iota(jnp.int32, (n, n), 0) == lax.broadcasted_iota(jnp.int32, (n, n), 1)
    ).astype(f32)


def eliminate(stack, n):
    m = stack.shape[1]
    row_at = lax.broadcasted_iota(jnp.int32, (n, m), 0)
    lane_at = lax.broadcasted_iota(jnp.int32, (n, m), 1)
    spread_column = lambda i: jnp.broadcast_to(stack[:, i : i + 1], (n, m))

    def solve_pair(j, one, two, lines):
        a, b, d = one[j : j + 1], two[j : j + 1], two[j + 1 : j + 2]
        over = 1.0 / (a * d - b * b)
        return [((d * u - b * v) * over, (a * v - b * u) * over) for u, v in lines]

    for j in range(0, n - 2, 4):
        one, two = spread_column(j), spread_column(j + 1)
        lines = [(stack[j : j + 1], stack[j + 1 : j + 2])]
        more = j + 4 < n
        if more:
            three, four = spread_column(j + 2), spread_column(j + 3)
            lines += [(c[j : j + 1], c[j + 1 : j + 2]) for c in (three, four)]
        (u, v), *at = solve_pair(j, one, two, lines)
        below = row_at > j + 1
        one, two = jnp.where(below, one, 0.0), jnp.where(below, two, 0.0)
        stack = stack - one * u - two * v
        if more:
            three, four = (c - one * p - two * q for c, (p, q) in zip((three, four), at))
            k = j + 2
            ((u, v),) = solve_pair(k, three, four, [(stack[k : k + 1], stack[k + 1 : k + 2])])
            below = row_at > k + 1
            stack = stack - jnp.where(below, three, 0.0) * u - jnp.where(below, four, 0.0) * v
    odd = row_at % 2 == 1
    above = jnp.concatenate([stack[n - 1 :], stack[: n - 1]], axis=0)
    pivot = jnp.sum(jnp.where(row_at == lane_at + 1, above, 0.0), axis=1, keepdims=True)
    beside = jnp.sum(jnp.where(row_at == lane_at + 1, stack, 0.0), axis=1, keepdims=True)
    ratio = beside / jnp.where(odd[:, :1], pivot, 1.0)
    stack = jnp.where(odd, stack - ratio * above, stack)
    diagonal = jnp.sum(jnp.where(row_at == lane_at, stack, 0.0), axis=1, keepdims=True)
    return stack / jnp.sqrt(diagonal)


def table_kernel(cols_ref, live_ref, table_ref):
    slot = lax.broadcasted_iota(jnp.int32, cols_ref.shape, 0)
    table_ref[...] = 2 * cols_ref[...] + (slot < live_ref[...]).astype(jnp.int32)


def place(table_ref, b, k, me_col, per_span, row_count):
    g = lax.shift_right_logical(table_ref[k, b], 1)
    span = lax.div(g, per_span)
    return (lax.div(span, row_count) ^ me_col) * per_span + lax.rem(g, per_span)


def mark_kernel(mark_ref):
    mark_ref[...] = jnp.zeros_like(mark_ref)


def stack_kernel(*refs):
    out_ref, at = refs[-1], 0
    for ref in refs[:-2]:
        array = ref[...]
        n = array.shape[0] if array.ndim == 3 else 1
        out_ref[at : at + n] = array.reshape((n,) + array.shape[-2:])
        at += n


def forward_kernel(sizes, table_ref, even_ref, odd_ref, *rest):
    row_count, col_count, _, width, bs = sizes
    x_refs = rest[:col_count]
    gram_ref, blocks_ref, begun_ref, p_ref, keep_ref, send_ref, extra_ref = rest[
        col_count : col_count + 7
    ]
    back_refs, picks, spread = rest[col_count + 7 : -2], rest[-2], rest[-1]
    per_span = keep_ref.shape[2] // bs
    me_col = lax.axis_index("col")
    me_row = lax.axis_index("row")
    for s in range(col_count):
        for o in range(per_span):
            picks[s * per_span + o] = split_rows(x_refs[s][:, o * bs : (o + 1) * bs])
    gram = gram_ref[...]
    spread[...] = begun_ref[...]
    n = odd_ref.shape[0]
    backward_spans(sizes, 1, table_ref, odd_ref, blocks_ref, spread, 0, n)
    for s, back_ref in enumerate(back_refs):
        for o in range(per_span):
            back_ref[:width, o * bs : (o + 1) * bs] = spread[s * per_span + o]
        back_ref[width:] = p_ref[...]

    def two_spans(h, cross):
        for i, (out_ref, rows_ref) in enumerate(((keep_ref, even_ref), (send_ref, odd_ref))):
            forward = forward_span(
                sizes, 2 * h + i, table_ref, picks, blocks_ref, per_span, me_row, me_col
            )
            out_ref[h] = forward
            cross = cross + three_pass(dot_nt, rows_ref[h], forward)
        return cross

    cross = lax.fori_loop(
        0, row_count // 2, two_spans, jnp.zeros((width, width), f32), unroll=UNROLL
    )
    extra_ref[...] = pack([gram[:width, :width], gram[:width, width:], gram[width:, width:], cross])


def forward_span(
    sizes, s, table_ref, picks, blocks_ref, per_span, me_row, me_col
):
    row_count, _, slots, _, _ = sizes
    n = picks.shape[1] // 2
    parts = []
    for o in range(per_span):
        b = (me_row ^ s) * per_span + o
        tiles, chosen = [], []
        for k in range(slots):
            w = (table_ref[k, b] & 1).astype(f32)
            at = place(table_ref, b, k, me_col, per_span, row_count)
            tiles.append(blocks_ref[b, k])
            chosen.append(picks[at] * w.astype(bf16))
        both = dot_nt(jnp.concatenate(chosen, axis=1), jnp.concatenate(tiles, axis=1), None)
        parts.append(both[:n] + both[n:])
    return jnp.concatenate(parts, axis=1)


def backward_spans(sizes, parity, table_ref, rows_ref, blocks_ref, spread, begin, end):
    row_count, _, slots, width, bs = sizes
    per_span = rows_ref.shape[2] // bs
    me_col = lax.axis_index("col")
    me_row = lax.axis_index("row")

    def one_span(h, carry):
        own = split_rows(rows_ref[h])
        for o in range(per_span):
            b = (me_row ^ (2 * h + parity)) * per_span + o
            tile = jnp.concatenate([blocks_ref[b, k] for k in range(slots)], axis=1)
            back = dot_nn(own[:, o * bs : (o + 1) * bs], tile, None)
            back = back[:width] + back[width:]
            for k in range(slots):
                at = place(table_ref, b, k, me_col, per_span, row_count)
                w = (table_ref[k, b] & 1).astype(f32)
                spread[at] += back[:, k * bs : (k + 1) * bs] * w
        return carry

    lax.fori_loop(begin, end, one_span, 0, unroll=min(UNROLL, end - begin))


def back_near_kernel(
    sizes, table_ref, near_ref, blocks_ref, p_ref, spread_ref, gram_ref
):
    spread_ref[...] = jnp.zeros_like(spread_ref)
    pair = jnp.concatenate([near_ref[0], p_ref[...]], axis=0)
    gram_ref[...] = four_pass(dot_nt, pair, pair)
    n = near_ref.shape[0]
    backward_spans(sizes, 0, table_ref, near_ref, blocks_ref, spread_ref, 0, n)


def back_even_kernel(
    sizes, near, table_ref, even_ref, blocks_ref, begun_ref, spread_ref
):
    spread_ref[...] = begun_ref[...]
    n = even_ref.shape[0]
    backward_spans(sizes, 0, table_ref, even_ref, blocks_ref, spread_ref, near, n)


def put(ref, vectors, extra):
    h, n = vectors.shape[0] // 2, vectors.shape[1]
    ref[:, :n] = vectors[:h]
    ref[:, n : 2 * n] = vectors[h:]
    ref[:, 2 * n :] = extra


def take(message):
    n = (message.shape[1] - LANES) // 2
    return jnp.concatenate([message[:, :n], message[:, n : 2 * n]], axis=0), message[:, 2 * n :]


def fold_kernel(keep_ref, got_ref, extra_ref, got_extra_ref, low_ref, high_ref):
    extra = extra_ref[...] + got_extra_ref[...]
    n = low_ref.shape[0]
    for i, out_ref in enumerate((low_ref, high_ref)):
        for h in range(n):
            put(out_ref.at[h], keep_ref[i * n + h] + got_ref[i * n + h], extra)


def fold_more_kernel(keep_ref, got_ref, low_ref, high_ref):
    n = low_ref.shape[0]
    low_ref[...] = keep_ref[:n] + got_ref[:n]
    high_ref[...] = keep_ref[n:] + got_ref[n:]


def tree_sum(terms):
    while len(terms) > 1:
        terms = [terms[i] + terms[i + 1] for i in range(0, len(terms), 2)]
    return terms[0]


def middle_kernel(col_count, keep_ref, got_ref, *refs):
    back_refs = refs[:col_count]
    out_ref, y_ref = refs[col_count:]
    width = y_ref.shape[0] // 2
    forward, sums = take(keep_ref[0] + got_ref[0])
    y = 0.5 * (forward + tree_sum([ref[:width] for ref in back_refs]))
    y_ref[:width] = y
    y_ref[width:] = back_refs[0][width:]
    put(out_ref, y, sums)


def solve(y_refs, aux_ref, w):
    sums = tree_sum([take(y_ref[...])[1] for y_ref in y_refs])
    gram_x, xp, pp, xbx = (unpack(sums, i) for i in range(4))
    cross_x = 0.5 * (xbx + xbx.T)
    done = eliminate(jnp.concatenate([gram_x, eye(w), cross_x, xp], axis=1), w)
    inverse_l, below_p = done[:, w : 2 * w], done[:, 3 * w : 4 * w]
    coefficient = dot_tn(inverse_l, done[:, 2 * w : 3 * w])
    minus_c_t = -coefficient.T
    aux_ref[...] = jnp.concatenate(
        [minus_c_t, coefficient, below_p, xp, pp, cross_x, inverse_l, gram_x], axis=1
    )
    return minus_c_t


def forward_rest_kernel(sizes, table_ref, *rest):
    row_count, col_count, _, width, bs = sizes
    y_refs, x_refs, p_refs = (rest[i * col_count : (i + 1) * col_count] for i in range(3))
    blocks_ref, out_ref, resid_ref, resid_out_ref, aux_ref, picks = rest[3 * col_count :]
    span_rows = out_ref.shape[2]
    per_span = span_rows // bs
    me_col = lax.axis_index("col")
    me_row = lax.axis_index("row")
    minus_c_t = solve(y_refs, aux_ref, width)
    for s in range(col_count):
        rest_s = take(y_refs[s][...])[0] + dot_nn(minus_c_t, x_refs[s][...])
        if s == 0:
            resid_ref[...] = rest_s
            resid_out_ref[...] = rest_s
        both = jnp.concatenate([rest_s, p_refs[s][width:]], axis=0)
        for o in range(per_span):
            picks[s * per_span + o] = split_rows(both[:, o * bs : (o + 1) * bs])

    def two_spans(h, carry):
        for s in (2 * h, 2 * h + 1):
            out_ref[s] = forward_span(
                sizes, s, table_ref, picks, blocks_ref, per_span, me_row, me_col
            )
        return carry

    lax.fori_loop(0, row_count // 2, two_spans, 0, unroll=UNROLL)


def iota(shape, axis):
    return lax.broadcasted_iota(jnp.int32, shape, axis)


def pack(matrices):
    h = matrices[0].shape[0] // 2
    return jnp.concatenate([part for m in matrices for part in (m[:h], m[h:])], axis=1)


def unpack(packed, i):
    w = 2 * packed.shape[0]
    at = 2 * i * w
    return jnp.concatenate([packed[:, at : at + w], packed[:, at + w : at + 2 * w]], axis=0)


def gram_spans(width, parity, aux_ref, x_ref, y_ref, forward_ref):
    w = width
    minus_c_t = aux_ref[:, :w]

    def two_spans(i, cross):
        for h in (2 * i, 2 * i + 1):
            rest_q = y_ref[h, :w, :] + three_pass(dot_nn, minus_c_t, x_ref[h])
            both = jnp.concatenate([rest_q, y_ref[h, w:, :]], axis=0)
            cross = cross + three_pass(dot_nt, both, forward_ref[2 * h + parity])
        return cross

    zero = jnp.zeros((2 * w, 2 * w), f32)
    return lax.fori_loop(0, x_ref.shape[0] // 2, two_spans, zero, unroll=UNROLL // 2)


def gram_even_kernel(
    width, aux_ref, x_ref, y_ref, forward_ref, p_ref, resid_ref, cross_ref, gram_ref, wide_ref
):
    w = width
    coefficient, below_p, cross_x, inverse_l, gram_x = (
        aux_ref[:, i * w : (i + 1) * w] for i in (1, 2, 5, 6, 7)
    )
    xr = cross_x - dot_nn(gram_x, coefficient)
    upper = jnp.concatenate([dot_nn(inverse_l, xr), below_p], axis=1)
    wide_ref[...] = jnp.concatenate(
        [
            dot_tn(upper, upper),
            -dot_tn(upper, inverse_l),
            jnp.concatenate([xr, jnp.zeros((w, w), f32)], axis=0),
        ],
        axis=1,
    )
    mine = resid_ref[...]
    gram_ref[...] = four_pass(dot_nt, mine, jnp.concatenate([mine, p_ref[...]], axis=0))
    cross_ref[...] = gram_spans(width, 0, aux_ref, x_ref, y_ref, forward_ref)


def gram_odd_kernel(width, aux_ref, x_ref, y_ref, forward_ref, cross_ref, gram_ref, part_ref):
    w = width
    gram = gram_ref[...]
    cross = cross_ref[...] + gram_spans(w, 1, aux_ref, x_ref, y_ref, forward_ref)
    rar, pap = cross[:w, :w], cross[w:, w:]
    rar = 0.5 * (rar + rar.T)
    pap = 0.5 * (pap + pap.T)
    rap = 0.5 * (cross[:w, w:] + cross[w:, :w].T)
    row, lane = iota((w, w), 0), iota((w, w), 1)
    diagonal = jnp.sum(jnp.where(row == lane, rar, 0.0), axis=1, keepdims=True)
    first = jnp.where(row <= lane, gram[:, :w], rar)
    corner = jnp.where((row == w - 1) & (lane == 1), diagonal[0:1, 0:1], 0.0)
    second = jnp.where(row <= lane, pap, jnp.where(lane == 0, diagonal, corner))
    part = pack([first, second, gram[:, w:], rap])
    for d in range(part_ref.shape[0]):
        part_ref[d] = part


def last_kernel(
    width, scale, parts_ref, aux_ref, wide_ref, x_ref, yp_ref, resid_ref, x_next_ref, reduced_ref
):
    w = width
    total = parts_ref[0]
    for d in range(1, parts_ref.shape[0]):
        total = total + parts_ref[d]
    first, second, rp, rap = (unpack(total, i) for i in range(4))
    row, lane = iota((w, w), 0), iota((w, w), 1)
    below = first.T
    diagonal = jnp.where(iota((w, 1), 0) == 0, second[w - 1 : w, 1:2], second[:, 0:1])
    rr = jnp.where(row <= lane, first, below)
    rar = jnp.where(row > lane, first, jnp.where(row < lane, below, diagonal))
    pap = jnp.where(row <= lane, second, second.T)
    coefficient, xp, pp, xax, inverse_x = (
        aux_ref[:, i * w : (i + 1) * w] for i in (1, 3, 4, 5, 6)
    )
    xr = wide_ref[:w, 3 * w : 4 * w]
    schur = (
        jnp.concatenate(
            [jnp.concatenate([rr, rp], axis=1), jnp.concatenate([rp.T, pp], axis=1)], axis=0
        )
        - wide_ref[:, : 2 * w]
    )
    xar = rr + dot_tn(coefficient, xr)
    xap = rp + dot_tn(coefficient, xp)
    gram_apply = jnp.concatenate(
        [
            jnp.concatenate([xax, xar, xap], axis=1),
            jnp.concatenate([xar.T, rar, rap], axis=1),
            jnp.concatenate([xap.T, rap.T, pap], axis=1),
        ],
        axis=0,
    )
    n = 3 * w
    rest = eliminate(
        jnp.concatenate([schur, eye(2 * w), wide_ref[:, 2 * w : 3 * w]], axis=1), 2 * w
    )
    inverse_l = jnp.concatenate(
        [
            jnp.concatenate([inverse_x, jnp.zeros((w, 2 * w), f32)], axis=1),
            jnp.concatenate([rest[:, 4 * w : 5 * w], rest[:, 2 * w : 4 * w]], axis=1),
        ],
        axis=0,
    )
    reduced = dot_nt(dot_nn(inverse_l, gram_apply), inverse_l)
    reduced_ref[...] = reduced
    shifted = reduced + 3.0 * eye(n)
    target = dot_nn(shifted, shifted[:, :w])
    gram_fresh = dot_tn(target, target)
    mixing = dot_tn(target, inverse_l)
    weights = scale * eliminate(jnp.concatenate([gram_fresh, mixing], axis=1), w)[:, w:]
    basis = jnp.concatenate([x_ref[0], resid_ref[...], yp_ref[w:, :]], axis=0)
    x_next_ref[...] = dot_nn(weights, basis)


def per_device(block_vecs, direction, blocks, block_cols, live_counts):
    row_count = lax.axis_size("row")
    col_count = lax.axis_size("col")
    width, span_rows = block_vecs.shape
    slots, bs = blocks.shape[1:3]
    per_span = span_rows // bs
    half = row_count // 2
    order_total = span_rows * row_count * col_count
    col_blocks = col_count * per_span
    sizes = (row_count, col_count, slots, width, bs)
    shape = lambda *dims: jax.ShapeDtypeStruct(dims, f32)
    spec = {
        "v": pl.BlockSpec(memory_space=VMEM),
        "s": pl.BlockSpec(memory_space=SMEM),
    }

    def call(kernel, ins, args, outs, scratch=(), cost=None):
        return pl.pallas_call(
            kernel,
            in_specs=[spec[letter] for letter in ins],
            out_specs=[spec["v"]] * len(outs),
            out_shape=outs,
            scratch_shapes=scratch,
            compiler_params=pltpu.CompilerParams(vmem_limit_bytes=VMEM_LIMIT),
            cost_estimate=cost,
        )(*args)

    def swap(array, axis, s):
        return lax.ppermute(array, axis, [(i, i ^ s) for i in range(lax.axis_size(axis))])

    far = list(reversed(range(1, col_count)))
    bits = row_bits(row_count)
    window = pl.CostEstimate(flops=LOAD_FLOPS, bytes_accessed=0, transcendentals=0)

    def gather_rows(array):
        even = array
        for bit in bits:
            got = swap(even, "row", bit)
            (even,) = call(stack_kernel, "vvv", [even, got, mark], [shape(bit, *array.shape)])
            if bit == bits[0]:
                near = even
        return near, even, swap(even, "row", 1)

    def over_col(arrays):
        got = {s: swap(arrays[s], "col", s) for s in far}
        return [arrays[0]] + [got[s] for s in range(1, col_count)]

    (mark,) = call(mark_kernel, "", [], [shape(8, LANES)], cost=window)
    (table,) = call(
        table_kernel,
        "vv",
        [block_cols.T, live_counts.T],
        [jax.ShapeDtypeStruct(block_cols.T.shape, jnp.int32)],
    )
    x_cols = over_col([block_vecs] * col_count)
    x_near, x_even, x_odd = gather_rows(block_vecs)
    begun, gram = call(
        functools.partial(back_near_kernel, sizes),
        "svvv",
        [table, x_near, blocks, direction],
        [shape(col_blocks, width, bs), shape(2 * width, 2 * width)],
    )
    if half > x_near.shape[0]:
        (begun,) = call(
            functools.partial(back_even_kernel, sizes, x_near.shape[0]),
            "svvv",
            [table, x_even, blocks, begun],
            [shape(col_blocks, width, bs)],
        )
    keep, send, extra, *backs = call(
        functools.partial(forward_kernel, sizes),
        "svv" + "v" * (col_count + 4),
        [table, x_even, x_odd, *x_cols, gram, blocks, begun, direction],
        [shape(half, width, span_rows)] * 2
        + [shape(width // 2, LANES)]
        + [shape(2 * width, span_rows)] * col_count,
        [
            pltpu.VMEM((col_blocks, 2 * width, bs), bf16),
            pltpu.VMEM((col_blocks, width, bs), f32),
        ],
    )
    got_pair = swap(send, "row", 1)
    got_extra = swap(extra, "row", 1)
    got_backs = over_col(backs)
    low, high = call(
        fold_kernel,
        "vvvv",
        [keep, got_pair, extra, got_extra],
        [shape(half // 2, width // 2, 2 * span_rows + LANES)] * 2,
    )
    for bit in reversed(bits):
        got = swap(high, "row", bit)
        if bit != bits[0]:
            low, high = call(
                fold_more_kernel,
                "vv",
                [low, got],
                [shape(low.shape[0] // 2, width // 2, 2 * span_rows + LANES)] * 2,
            )
    message, image = call(
        functools.partial(middle_kernel, col_count),
        "v" * (2 + col_count),
        [low, got, *got_backs],
        [shape(width // 2, 2 * span_rows + LANES), shape(2 * width, span_rows)],
    )
    image_cols = over_col([message] * col_count)
    _, image_even, image_odd = gather_rows(image)
    forward_rp, resid, resid_out, aux = call(
        functools.partial(forward_rest_kernel, sizes),
        "s" + "v" * (3 * col_count + 1),
        [table, *image_cols, *x_cols, *got_backs, blocks],
        [shape(row_count, 2 * width, span_rows)]
        + [shape(width, span_rows)] * 2
        + [shape(width, 8 * width)],
        [pltpu.VMEM((col_blocks, 4 * width, bs), bf16)],
    )
    cross, gram, wide = call(
        functools.partial(gram_even_kernel, width),
        "v" * 6,
        [aux, x_even, image_even, forward_rp, direction, resid],
        [shape(2 * width, 2 * width), shape(width, 2 * width), shape(2 * width, 4 * width)],
    )
    (part,) = call(
        functools.partial(gram_odd_kernel, width),
        "v" * 6,
        [aux, x_odd, image_odd, forward_rp, cross, gram],
        [shape(row_count * col_count, width // 2, LANES)],
    )
    parts = lax.all_to_all(part, ("col", "row"), 0, 0)
    x_next, reduced = call(
        functools.partial(last_kernel, width, math.sqrt(order_total)),
        "v" * 6,
        [parts, aux, wide, x_even, image, resid],
        [shape(width, span_rows), shape(3 * width, 3 * width)],
    )
    return (x_next, reduced, resid_out)


def row_bits(row_count):
    return [1 << i for i in range(1, row_count.bit_length() - 1)]


def solution(mesh):
    return jax.shard_map(
        per_device,
        mesh=mesh,
        in_specs=(
            P(None, ("col", "row")),
            P(None, ("col", "row")),
            P("col", "row", None, None),
            P("col", "row"),
            P("col", "row"),
        ),
        out_specs=(P(None, ("col", "row")), P(), P(None, ("col", "row"))),
        check_vma=False,
    )
```

```python
import functools
import math

import jax
import jax.numpy as jnp
from jax import lax
from jax.experimental import pallas as pl
from jax.experimental.pallas import tpu as pltpu
from jax.sharding import PartitionSpec as P


highest = lax.Precision.HIGHEST
f32 = jnp.float32
bf16 = jnp.bfloat16
VMEM = pltpu.MemorySpace.VMEM
SMEM = pltpu.MemorySpace.SMEM
LANES = 128
VMEM_LIMIT = 16 * 1024 * 1024
UNROLL = 4
LOAD_FLOPS = 20_000_000_000


def dot_nt(a, b, precision=highest):
    return lax.dot_general(
        a, b, (((1,), (1,)), ((), ())), precision=precision, preferred_element_type=f32
    )


def dot_nn(a, b, precision=highest):
    return lax.dot_general(
        a, b, (((1,), (0,)), ((), ())), precision=precision, preferred_element_type=f32
    )


def dot_tn(a, b, precision=highest):
    return lax.dot_general(
        a, b, (((0,), (0,)), ((), ())), precision=precision, preferred_element_type=f32
    )


def split(x):
    hi = x.astype(bf16)
    lo = (x - hi.astype(f32)).astype(bf16)
    return hi, lo


def split_rows(x):
    hi, lo = split(x)
    return jnp.concatenate([hi, lo], axis=0)


def three_pass(dot, a, b):
    a_hi, a_lo = split(a)
    b_hi, b_lo = split(b)
    n = a.shape[0]
    top = dot(jnp.concatenate([a_hi, a_lo], axis=0), b_hi, None)
    return top[:n] + top[n:] + dot(a_hi, b_lo, None)


def four_pass(dot, a, b):
    b_hi, b_lo = split(b)
    n = a.shape[0]
    both = split_rows(a)
    top, low = dot(both, b_hi, None), dot(both, b_lo, None)
    return top[:n] + (top[n:] + low[:n] + low[n:])


def eye(n):
    return (
        lax.broadcasted_iota(jnp.int32, (n, n), 0) == lax.broadcasted_iota(jnp.int32, (n, n), 1)
    ).astype(f32)


def eliminate(stack, n):
    m = stack.shape[1]
    row_at = lax.broadcasted_iota(jnp.int32, (n, m), 0)
    lane_at = lax.broadcasted_iota(jnp.int32, (n, m), 1)
    spread_column = lambda i: jnp.broadcast_to(stack[:, i : i + 1], (n, m))

    def solve_pair(j, one, two, lines):
        a, b, d = one[j : j + 1], two[j : j + 1], two[j + 1 : j + 2]
        over = 1.0 / (a * d - b * b)
        return [((d * u - b * v) * over, (a * v - b * u) * over) for u, v in lines]

    for j in range(0, n - 2, 4):
        one, two = spread_column(j), spread_column(j + 1)
        lines = [(stack[j : j + 1], stack[j + 1 : j + 2])]
        more = j + 4 < n
        if more:
            three, four = spread_column(j + 2), spread_column(j + 3)
            lines += [(c[j : j + 1], c[j + 1 : j + 2]) for c in (three, four)]
        (u, v), *at = solve_pair(j, one, two, lines)
        below = row_at > j + 1
        one, two = jnp.where(below, one, 0.0), jnp.where(below, two, 0.0)
        stack = stack - one * u - two * v
        if more:
            three, four = (c - one * p - two * q for c, (p, q) in zip((three, four), at))
            k = j + 2
            ((u, v),) = solve_pair(k, three, four, [(stack[k : k + 1], stack[k + 1 : k + 2])])
            below = row_at > k + 1
            stack = stack - jnp.where(below, three, 0.0) * u - jnp.where(below, four, 0.0) * v
    odd = row_at % 2 == 1
    above = jnp.concatenate([stack[n - 1 :], stack[: n - 1]], axis=0)
    pivot = jnp.sum(jnp.where(row_at == lane_at + 1, above, 0.0), axis=1, keepdims=True)
    beside = jnp.sum(jnp.where(row_at == lane_at + 1, stack, 0.0), axis=1, keepdims=True)
    ratio = beside / jnp.where(odd[:, :1], pivot, 1.0)
    stack = jnp.where(odd, stack - ratio * above, stack)
    diagonal = jnp.sum(jnp.where(row_at == lane_at, stack, 0.0), axis=1, keepdims=True)
    return stack / jnp.sqrt(diagonal)


def table_kernel(cols_ref, live_ref, table_ref):
    slot = lax.broadcasted_iota(jnp.int32, cols_ref.shape, 0)
    table_ref[...] = 2 * cols_ref[...] + (slot < live_ref[...]).astype(jnp.int32)


def place(table_ref, b, k, me_col, per_span, row_count):
    g = lax.shift_right_logical(table_ref[k, b], 1)
    span = lax.div(g, per_span)
    return (lax.div(span, row_count) ^ me_col) * per_span + lax.rem(g, per_span)


def mark_kernel(mark_ref):
    mark_ref[...] = jnp.zeros_like(mark_ref)


def stack_kernel(*refs):
    out_ref, at = refs[-1], 0
    for ref in refs[:-2]:
        array = ref[...]
        n = array.shape[0] if array.ndim == 3 else 1
        out_ref[at : at + n] = array.reshape((n,) + array.shape[-2:])
        at += n


def forward_kernel(sizes, table_ref, even_ref, odd_ref, *rest):
    row_count, col_count, _, width, bs = sizes
    x_refs = rest[:col_count]
    gram_ref, blocks_ref, begun_ref, p_ref, keep_ref, send_ref, extra_ref = rest[
        col_count : col_count + 7
    ]
    back_refs, picks, spread = rest[col_count + 7 : -2], rest[-2], rest[-1]
    per_span = keep_ref.shape[2] // bs
    me_col = lax.axis_index("col")
    me_row = lax.axis_index("row")
    for s in range(col_count):
        for o in range(per_span):
            picks[s * per_span + o] = split_rows(x_refs[s][:, o * bs : (o + 1) * bs])
    gram = gram_ref[...]
    spread[...] = begun_ref[...]
    n = odd_ref.shape[0]
    backward_spans(sizes, 1, table_ref, odd_ref, blocks_ref, spread, 0, n)
    for s, back_ref in enumerate(back_refs):
        for o in range(per_span):
            back_ref[:width, o * bs : (o + 1) * bs] = spread[s * per_span + o]
        back_ref[width:] = p_ref[...]

    def two_spans(h, cross):
        for i, (out_ref, rows_ref) in enumerate(((keep_ref, even_ref), (send_ref, odd_ref))):
            forward = forward_span(
                sizes, 2 * h + i, table_ref, picks, blocks_ref, per_span, me_row, me_col
            )
            out_ref[h] = forward
            cross = cross + three_pass(dot_nt, rows_ref[h], forward)
        return cross

    cross = lax.fori_loop(
        0, row_count // 2, two_spans, jnp.zeros((width, width), f32), unroll=UNROLL
    )
    extra_ref[...] = pack([gram[:width, :width], gram[:width, width:], gram[width:, width:], cross])


def forward_span(
    sizes, s, table_ref, picks, blocks_ref, per_span, me_row, me_col
):
    row_count, _, slots, _, _ = sizes
    n = picks.shape[1] // 2
    parts = []
    for o in range(per_span):
        b = (me_row ^ s) * per_span + o
        tiles, chosen = [], []
        for k in range(slots):
            w = (table_ref[k, b] & 1).astype(f32)
            at = place(table_ref, b, k, me_col, per_span, row_count)
            tiles.append(blocks_ref[b, k])
            chosen.append(picks[at] * w.astype(bf16))
        both = dot_nt(jnp.concatenate(chosen, axis=1), jnp.concatenate(tiles, axis=1), None)
        parts.append(both[:n] + both[n:])
    return jnp.concatenate(parts, axis=1)


def backward_spans(sizes, parity, table_ref, rows_ref, blocks_ref, spread, begin, end):
    row_count, _, slots, width, bs = sizes
    per_span = rows_ref.shape[2] // bs
    me_col = lax.axis_index("col")
    me_row = lax.axis_index("row")

    def one_span(h, carry):
        own = split_rows(rows_ref[h])
        for o in range(per_span):
            b = (me_row ^ (2 * h + parity)) * per_span + o
            tile = jnp.concatenate([blocks_ref[b, k] for k in range(slots)], axis=1)
            back = dot_nn(own[:, o * bs : (o + 1) * bs], tile, None)
            back = back[:width] + back[width:]
            for k in range(slots):
                at = place(table_ref, b, k, me_col, per_span, row_count)
                w = (table_ref[k, b] & 1).astype(f32)
                spread[at] += back[:, k * bs : (k + 1) * bs] * w
        return carry

    lax.fori_loop(begin, end, one_span, 0, unroll=min(UNROLL, end - begin))


def back_near_kernel(
    sizes, table_ref, near_ref, blocks_ref, p_ref, spread_ref, gram_ref
):
    spread_ref[...] = jnp.zeros_like(spread_ref)
    pair = jnp.concatenate([near_ref[0], p_ref[...]], axis=0)
    gram_ref[...] = four_pass(dot_nt, pair, pair)
    n = near_ref.shape[0]
    backward_spans(sizes, 0, table_ref, near_ref, blocks_ref, spread_ref, 0, n)


def back_even_kernel(
    sizes, near, table_ref, even_ref, blocks_ref, begun_ref, spread_ref
):
    spread_ref[...] = begun_ref[...]
    n = even_ref.shape[0]
    backward_spans(sizes, 0, table_ref, even_ref, blocks_ref, spread_ref, near, n)


def put(ref, vectors, extra):
    h, n = vectors.shape[0] // 2, vectors.shape[1]
    ref[:, :n] = vectors[:h]
    ref[:, n : 2 * n] = vectors[h:]
    ref[:, 2 * n :] = extra


def take(message):
    n = (message.shape[1] - LANES) // 2
    return jnp.concatenate([message[:, :n], message[:, n : 2 * n]], axis=0), message[:, 2 * n :]


def fold_kernel(keep_ref, got_ref, extra_ref, got_extra_ref, low_ref, high_ref):
    extra = extra_ref[...] + got_extra_ref[...]
    n = low_ref.shape[0]
    for i, out_ref in enumerate((low_ref, high_ref)):
        for h in range(n):
            put(out_ref.at[h], keep_ref[i * n + h] + got_ref[i * n + h], extra)


def fold_more_kernel(keep_ref, got_ref, low_ref, high_ref):
    n = low_ref.shape[0]
    low_ref[...] = keep_ref[:n] + got_ref[:n]
    high_ref[...] = keep_ref[n:] + got_ref[n:]


def tree_sum(terms):
    while len(terms) > 1:
        terms = [terms[i] + terms[i + 1] for i in range(0, len(terms), 2)]
    return terms[0]


def middle_kernel(col_count, keep_ref, got_ref, *refs):
    back_refs = refs[:col_count]
    out_ref, y_ref = refs[col_count:]
    width = y_ref.shape[0] // 2
    forward, sums = take(keep_ref[0] + got_ref[0])
    y = 0.5 * (forward + tree_sum([ref[:width] for ref in back_refs]))
    y_ref[:width] = y
    y_ref[width:] = back_refs[0][width:]
    put(out_ref, y, sums)


def solve(y_refs, aux_ref, w):
    sums = tree_sum([take(y_ref[...])[1] for y_ref in y_refs])
    gram_x, xp, pp, xbx = (unpack(sums, i) for i in range(4))
    cross_x = 0.5 * (xbx + xbx.T)
    done = eliminate(jnp.concatenate([gram_x, eye(w), cross_x, xp], axis=1), w)
    inverse_l, below_p = done[:, w : 2 * w], done[:, 3 * w : 4 * w]
    coefficient = dot_tn(inverse_l, done[:, 2 * w : 3 * w])
    minus_c_t = -coefficient.T
    aux_ref[...] = jnp.concatenate(
        [minus_c_t, coefficient, below_p, xp, pp, cross_x, inverse_l, gram_x], axis=1
    )
    return minus_c_t


def forward_rest_kernel(sizes, table_ref, *rest):
    row_count, col_count, _, width, bs = sizes
    y_refs, x_refs, p_refs = (rest[i * col_count : (i + 1) * col_count] for i in range(3))
    blocks_ref, out_ref, resid_ref, resid_out_ref, aux_ref, picks = rest[3 * col_count :]
    span_rows = out_ref.shape[2]
    per_span = span_rows // bs
    me_col = lax.axis_index("col")
    me_row = lax.axis_index("row")
    w = width
    for s in range(col_count):
        hi, lo = split(p_refs[s][w:])
        for o in range(per_span):
            picks[s * per_span + o, w : 2 * w] = hi[:, o * bs : (o + 1) * bs]
            picks[s * per_span + o, 3 * w :] = lo[:, o * bs : (o + 1) * bs]
    minus_c_t = solve(y_refs, aux_ref, width)
    for s in range(col_count):
        rest_s = take(y_refs[s][...])[0] + dot_nn(minus_c_t, x_refs[s][...])
        if s == 0:
            resid_ref[...] = rest_s
            resid_out_ref[...] = rest_s
        hi, lo = split(rest_s)
        for o in range(per_span):
            picks[s * per_span + o, :w] = hi[:, o * bs : (o + 1) * bs]
            picks[s * per_span + o, 2 * w : 3 * w] = lo[:, o * bs : (o + 1) * bs]

    def two_spans(h, carry):
        for s in (2 * h, 2 * h + 1):
            out_ref[s] = forward_span(
                sizes, s, table_ref, picks, blocks_ref, per_span, me_row, me_col
            )
        return carry

    lax.fori_loop(0, row_count // 2, two_spans, 0, unroll=UNROLL)


def iota(shape, axis):
    return lax.broadcasted_iota(jnp.int32, shape, axis)


def pack(matrices):
    h = matrices[0].shape[0] // 2
    return jnp.concatenate([part for m in matrices for part in (m[:h], m[h:])], axis=1)


def unpack(packed, i):
    w = 2 * packed.shape[0]
    at = 2 * i * w
    return jnp.concatenate([packed[:, at : at + w], packed[:, at + w : at + 2 * w]], axis=0)


def gram_spans(width, parity, aux_ref, x_ref, y_ref, forward_ref):
    w = width
    minus_c_t = aux_ref[:, :w]

    def two_spans(i, cross):
        for h in (2 * i, 2 * i + 1):
            rest_q = y_ref[h, :w, :] + three_pass(dot_nn, minus_c_t, x_ref[h])
            both = jnp.concatenate([rest_q, y_ref[h, w:, :]], axis=0)
            cross = cross + three_pass(dot_nt, both, forward_ref[2 * h + parity])
        return cross

    zero = jnp.zeros((2 * w, 2 * w), f32)
    return lax.fori_loop(0, x_ref.shape[0] // 2, two_spans, zero, unroll=UNROLL // 2)


def gram_even_kernel(
    width, aux_ref, x_ref, y_ref, forward_ref, p_ref, resid_ref, cross_ref, gram_ref, wide_ref
):
    w = width
    coefficient, below_p, cross_x, inverse_l, gram_x = (
        aux_ref[:, i * w : (i + 1) * w] for i in (1, 2, 5, 6, 7)
    )
    xr = cross_x - dot_nn(gram_x, coefficient)
    upper = jnp.concatenate([dot_nn(inverse_l, xr), below_p], axis=1)
    wide_ref[...] = jnp.concatenate(
        [
            dot_tn(upper, upper),
            -dot_tn(upper, inverse_l),
            jnp.concatenate([xr, jnp.zeros((w, w), f32)], axis=0),
        ],
        axis=1,
    )
    mine = resid_ref[...]
    gram_ref[...] = four_pass(dot_nt, mine, jnp.concatenate([mine, p_ref[...]], axis=0))
    cross_ref[...] = gram_spans(width, 0, aux_ref, x_ref, y_ref, forward_ref)


def gram_odd_kernel(width, aux_ref, x_ref, y_ref, forward_ref, cross_ref, gram_ref, part_ref):
    w = width
    gram = gram_ref[...]
    cross = cross_ref[...] + gram_spans(w, 1, aux_ref, x_ref, y_ref, forward_ref)
    rar, pap = cross[:w, :w], cross[w:, w:]
    rar = 0.5 * (rar + rar.T)
    pap = 0.5 * (pap + pap.T)
    rap = 0.5 * (cross[:w, w:] + cross[w:, :w].T)
    row, lane = iota((w, w), 0), iota((w, w), 1)
    diagonal = jnp.sum(jnp.where(row == lane, rar, 0.0), axis=1, keepdims=True)
    first = jnp.where(row <= lane, gram[:, :w], rar)
    corner = jnp.where((row == w - 1) & (lane == 1), diagonal[0:1, 0:1], 0.0)
    second = jnp.where(row <= lane, pap, jnp.where(lane == 0, diagonal, corner))
    part = pack([first, second, gram[:, w:], rap])
    for d in range(part_ref.shape[0]):
        part_ref[d] = part


def last_kernel(
    width, scale, parts_ref, aux_ref, wide_ref, x_ref, yp_ref, resid_ref, x_next_ref, reduced_ref
):
    w = width
    total = parts_ref[0]
    for d in range(1, parts_ref.shape[0]):
        total = total + parts_ref[d]
    first, second, rp, rap = (unpack(total, i) for i in range(4))
    row, lane = iota((w, w), 0), iota((w, w), 1)
    below = first.T
    diagonal = jnp.where(iota((w, 1), 0) == 0, second[w - 1 : w, 1:2], second[:, 0:1])
    rr = jnp.where(row <= lane, first, below)
    rar = jnp.where(row > lane, first, jnp.where(row < lane, below, diagonal))
    pap = jnp.where(row <= lane, second, second.T)
    coefficient, xp, pp, xax, inverse_x = (
        aux_ref[:, i * w : (i + 1) * w] for i in (1, 3, 4, 5, 6)
    )
    xr = wide_ref[:w, 3 * w : 4 * w]
    schur = (
        jnp.concatenate(
            [jnp.concatenate([rr, rp], axis=1), jnp.concatenate([rp.T, pp], axis=1)], axis=0
        )
        - wide_ref[:, : 2 * w]
    )
    xar = rr + dot_tn(coefficient, xr)
    xap = rp + dot_tn(coefficient, xp)
    gram_apply = jnp.concatenate(
        [
            jnp.concatenate([xax, xar, xap], axis=1),
            jnp.concatenate([xar.T, rar, rap], axis=1),
            jnp.concatenate([xap.T, rap.T, pap], axis=1),
        ],
        axis=0,
    )
    n = 3 * w
    rest = eliminate(
        jnp.concatenate([schur, eye(2 * w), wide_ref[:, 2 * w : 3 * w]], axis=1), 2 * w
    )
    inverse_l = jnp.concatenate(
        [
            jnp.concatenate([inverse_x, jnp.zeros((w, 2 * w), f32)], axis=1),
            jnp.concatenate([rest[:, 4 * w : 5 * w], rest[:, 2 * w : 4 * w]], axis=1),
        ],
        axis=0,
    )
    reduced = dot_nt(dot_nn(inverse_l, gram_apply), inverse_l)
    reduced_ref[...] = reduced
    shifted = reduced + 3.0 * eye(n)
    target = dot_nn(shifted, shifted[:, :w])
    gram_fresh = dot_tn(target, target)
    mixing = dot_tn(target, inverse_l)
    weights = scale * eliminate(jnp.concatenate([gram_fresh, mixing], axis=1), w)[:, w:]
    basis = jnp.concatenate([x_ref[0], resid_ref[...], yp_ref[w:, :]], axis=0)
    x_next_ref[...] = dot_nn(weights, basis)


def per_device(block_vecs, direction, blocks, block_cols, live_counts):
    row_count = lax.axis_size("row")
    col_count = lax.axis_size("col")
    width, span_rows = block_vecs.shape
    slots, bs = blocks.shape[1:3]
    per_span = span_rows // bs
    half = row_count // 2
    order_total = span_rows * row_count * col_count
    col_blocks = col_count * per_span
    sizes = (row_count, col_count, slots, width, bs)
    shape = lambda *dims: jax.ShapeDtypeStruct(dims, f32)
    spec = {
        "v": pl.BlockSpec(memory_space=VMEM),
        "s": pl.BlockSpec(memory_space=SMEM),
    }

    def call(kernel, ins, args, outs, scratch=(), cost=None):
        return pl.pallas_call(
            kernel,
            in_specs=[spec[letter] for letter in ins],
            out_specs=[spec["v"]] * len(outs),
            out_shape=outs,
            scratch_shapes=scratch,
            compiler_params=pltpu.CompilerParams(vmem_limit_bytes=VMEM_LIMIT),
            cost_estimate=cost,
        )(*args)

    def swap(array, axis, s):
        return lax.ppermute(array, axis, [(i, i ^ s) for i in range(lax.axis_size(axis))])

    far = list(reversed(range(1, col_count)))
    bits = row_bits(row_count)
    window = pl.CostEstimate(flops=LOAD_FLOPS, bytes_accessed=0, transcendentals=0)

    def gather_rows(array):
        even = array
        for bit in bits:
            got = swap(even, "row", bit)
            (even,) = call(stack_kernel, "vvv", [even, got, mark], [shape(bit, *array.shape)])
            if bit == bits[0]:
                near = even
        return near, even, swap(even, "row", 1)

    def over_col(arrays):
        got = {s: swap(arrays[s], "col", s) for s in far}
        return [arrays[0]] + [got[s] for s in range(1, col_count)]

    (mark,) = call(mark_kernel, "", [], [shape(8, LANES)], cost=window)
    (table,) = call(
        table_kernel,
        "vv",
        [block_cols.T, live_counts.T],
        [jax.ShapeDtypeStruct(block_cols.T.shape, jnp.int32)],
    )
    x_cols = over_col([block_vecs] * col_count)
    x_near, x_even, x_odd = gather_rows(block_vecs)
    begun, gram = call(
        functools.partial(back_near_kernel, sizes),
        "svvv",
        [table, x_near, blocks, direction],
        [shape(col_blocks, width, bs), shape(2 * width, 2 * width)],
    )
    if half > x_near.shape[0]:
        (begun,) = call(
            functools.partial(back_even_kernel, sizes, x_near.shape[0]),
            "svvv",
            [table, x_even, blocks, begun],
            [shape(col_blocks, width, bs)],
        )
    keep, send, extra, *backs = call(
        functools.partial(forward_kernel, sizes),
        "svv" + "v" * (col_count + 4),
        [table, x_even, x_odd, *x_cols, gram, blocks, begun, direction],
        [shape(half, width, span_rows)] * 2
        + [shape(width // 2, LANES)]
        + [shape(2 * width, span_rows)] * col_count,
        [
            pltpu.VMEM((col_blocks, 2 * width, bs), bf16),
            pltpu.VMEM((col_blocks, width, bs), f32),
        ],
    )
    got_pair = swap(send, "row", 1)
    got_extra = swap(extra, "row", 1)
    got_backs = over_col(backs)
    low, high = call(
        fold_kernel,
        "vvvv",
        [keep, got_pair, extra, got_extra],
        [shape(half // 2, width // 2, 2 * span_rows + LANES)] * 2,
    )
    for bit in reversed(bits):
        got = swap(high, "row", bit)
        if bit != bits[0]:
            low, high = call(
                fold_more_kernel,
                "vv",
                [low, got],
                [shape(low.shape[0] // 2, width // 2, 2 * span_rows + LANES)] * 2,
            )
    message, image = call(
        functools.partial(middle_kernel, col_count),
        "v" * (2 + col_count),
        [low, got, *got_backs],
        [shape(width // 2, 2 * span_rows + LANES), shape(2 * width, span_rows)],
    )
    image_cols = over_col([message] * col_count)
    _, image_even, image_odd = gather_rows(image)
    forward_rp, resid, resid_out, aux = call(
        functools.partial(forward_rest_kernel, sizes),
        "s" + "v" * (3 * col_count + 1),
        [table, *image_cols, *x_cols, *got_backs, blocks],
        [shape(row_count, 2 * width, span_rows)]
        + [shape(width, span_rows)] * 2
        + [shape(width, 8 * width)],
        [pltpu.VMEM((col_blocks, 4 * width, bs), bf16)],
    )
    cross, gram, wide = call(
        functools.partial(gram_even_kernel, width),
        "v" * 6,
        [aux, x_even, image_even, forward_rp, direction, resid],
        [shape(2 * width, 2 * width), shape(width, 2 * width), shape(2 * width, 4 * width)],
    )
    (part,) = call(
        functools.partial(gram_odd_kernel, width),
        "v" * 6,
        [aux, x_odd, image_odd, forward_rp, cross, gram],
        [shape(row_count * col_count, width // 2, LANES)],
    )
    parts = lax.all_to_all(part, ("col", "row"), 0, 0)
    x_next, reduced = call(
        functools.partial(last_kernel, width, math.sqrt(order_total)),
        "v" * 6,
        [parts, aux, wide, x_even, image, resid],
        [shape(width, span_rows), shape(3 * width, 3 * width)],
    )
    return (x_next, reduced, resid_out)


def row_bits(row_count):
    return [1 << i for i in range(1, row_count.bit_length() - 1)]


def solution(mesh):
    return jax.shard_map(
        per_device,
        mesh=mesh,
        in_specs=(
            P(None, ("col", "row")),
            P(None, ("col", "row")),
            P("col", "row", None, None),
            P("col", "row"),
            P("col", "row"),
        ),
        out_specs=(P(None, ("col", "row")), P(), P(None, ("col", "row"))),
        check_vma=False,
    )
```
